512 devices in a mesh: band: 4 (over x), grp: 16 (over y, z_hi), row: 8 (over z_lo, core).
Axes of the slice: x: 4, y: 4, z: 16 (z_hi: 4, z_lo: 4; z = z_hi * 4 + z_lo), core: 2. Of those that a mesh axis runs over, the one named last changes fastest.
Arguments:
- kspace_data: float32 [16, 16, 2, 2048], P('grp', 'row'), may hold values from -6 to 6
- coil_maps: bfloat16 [4, 16, 16, 256, 512], P('band', 'grp', 'row'), may hold values from -1.5 to 1.5
- smooth_weight: float32 [4, 16, 256, 256], P('band', 'grp', 'row'), may hold values from 0.3 to 3
- kernel_cols: bfloat16 [2048, 16], replicated, may hold values from -1.5 to 1.5
- kernel_rows: bfloat16 [2048, 16], replicated, may hold values from -1.5 to 1.5
- tile_index: int32 [16], replicated, may hold values from 0 to 255
- caipi_cycle: int32 [4], P('band'), may hold values from 0 to 3
Outputs:
- solution_field: float32 [4, 16, 256, 512], P('band', 'grp', 'row')
- residual: float32 [4, 16, 256, 512], P('band', 'grp', 'row')
The draws below stay inside these ranges and needn't reach their ends.
All inputs are finite; a program needn't handle non-finite values.
Results may differ from the reference program's by a relative error of at most 0.0003.
Values sent between devices are 32-bit elements; how exact they have to be, the bound alone decides.
A program may use at most 64 MiB of HBM per device.

```python
import math
import jax
import jax.numpy as jnp
from jax import lax

NY = 256
NX = 256
COILS = 16
TY = 16
TX = 16
SB = 128
NBLK = 16
ITERS = 1
MB = 4
GROUPS = 16
NTILES = 256
SAMPLES = 2048


def draw_coil_maps(key, part):
    shape = (MB, GROUPS, COILS, NY, 2 * NX)
    row_place = jnp.arange(NY, dtype=jnp.float32) / (NY - 1)
    slice_place = jnp.arange(MB, dtype=jnp.float32) / max(MB - 1, 1)
    ramp = (0.5 + row_place)[None, None, None, :, None] * (0.6 + 0.8 * slice_place)[:, None, None, None, None]
    values = 0.25 * ramp * jax.random.normal(key, shape, jnp.float32)
    return jnp.clip(values, -1.5, 1.5).astype(jnp.bfloat16)


def draw_kspace_data(key, part):
    shape = (GROUPS, COILS, 2, SAMPLES)
    group_place = jnp.arange(GROUPS, dtype=jnp.float32) / max(GROUPS - 1, 1)
    ramp = (0.5 + group_place)[:, None, None, None]
    values = ramp * jax.random.normal(key, shape, jnp.float32)
    return jnp.clip(values, -6.0, 6.0)


def set_ends(entries, key, least, largest):
    shape = entries.shape
    place = [jax.random.randint(jax.random.fold_in(key, axis), (), 0, shape[axis]) for axis in range(len(shape))]
    entries = entries.at[tuple(place)].set(least)
    longest = shape.index(max(shape))
    place[longest] = (place[longest] + 1) % shape[longest]
    return entries.at[tuple(place)].set(largest)


def block_scale(key, dims, pieces, low, top_value):
    gain = 1.0
    for position, shards_of in pieces:
        draws = jax.random.uniform(jax.random.fold_in(jax.random.fold_in(key, 6), position), (shards_of,), jnp.float32, low / len(pieces), top_value / len(pieces))
        gain = gain * jnp.repeat(jnp.exp(draws), dims[position] // shards_of).reshape((-1,) + (1,) * (len(dims) - 1 - position))
    return gain


def normal_values(own_key, dims, scale, reach, held_as=jnp.bfloat16):
    return jnp.clip(scale * jax.random.normal(own_key, dims, jnp.float32), -reach, reach).astype(held_as)


def setup_inputs(seed: int = 0) -> dict:
    key_list = jax.random.split(jax.random.key(seed), 8)
    kspace_data = draw_kspace_data(jax.random.fold_in(key_list[7], 71), 0)
    coil_maps = draw_coil_maps(jax.random.fold_in(key_list[7], 71), 0)
    smooth_weight = jnp.clip(jnp.exp(math.log(3.0) - 2.3025851 * jax.random.uniform(key_list[2], (MB, GROUPS, NY, NX), jnp.float32) ** block_scale(key_list[2], (MB, GROUPS, NY, NX), ((0, 4), (1, 16), (2, 8)), -0.2, 0.2)), 0.3, 3.0)
    kernel_cols = normal_values(key_list[3], (SAMPLES, TX), TX ** -0.5, 1.5)
    kernel_rows = normal_values(key_list[4], (SAMPLES, TY), TY ** -0.5, 1.5)
    tile_index = set_ends(jax.random.randint(key_list[5], (NBLK,), 0, NTILES), jax.random.fold_in(key_list[5], 1), 0, NTILES - 1).astype(jnp.int32)
    caipi_cycle = set_ends(jax.random.randint(key_list[6], (MB,), 0, MB), jax.random.fold_in(key_list[6], 1), 0, MB - 1).astype(jnp.int32)
    return dict(kspace_data=kspace_data, coil_maps=coil_maps, smooth_weight=smooth_weight, kernel_cols=kernel_cols, kernel_rows=kernel_rows, tile_index=tile_index, caipi_cycle=caipi_cycle)


reg_strength = 0.5
damping = 1.0
two_pi = 6.283185307179586
highest = lax.Precision.HIGHEST


def to_tiles(grid):
    count = grid.shape[0]
    shaped = grid.reshape(count, NY // TY, TY, 2, NX // TX, TX)
    return shaped.transpose(1, 4, 0, 3, 2, 5).reshape(NTILES, count * 2, TY, TX)


def from_tiles(tiles, count):
    shaped = tiles.reshape(NY // TY, NX // TX, count, 2, TY, TX)
    return shaped.transpose(2, 0, 4, 3, 1, 5).reshape(count, NY, 2 * NX)


def coil_images(profiles, image):
    profile = profiles.astype(jnp.float32)
    width = image.shape[-1] // 2
    coil_real, coil_imag = profile[..., :width], profile[..., width:]
    image_real, image_imag = image[None, :, :width], image[None, :, width:]
    return jnp.concatenate([coil_real * image_real - coil_imag * image_imag, coil_real * image_imag + coil_imag * image_real], axis=-1)


def combine_coils(profiles, images):
    profile = profiles.astype(jnp.float32)
    width = images.shape[-1] // 2
    coil_real, coil_imag = profile[..., :width], profile[..., width:]
    image_real, image_imag = images[..., :width], images[..., width:]
    real_sum = jnp.sum(coil_real * image_real + coil_imag * image_imag, axis=0)
    imag_sum = jnp.sum(coil_real * image_imag - coil_imag * image_real, axis=0)
    return jnp.concatenate([real_sum, imag_sum], axis=-1)


def to_complex(values):
    width = values.shape[-1] // 2
    return lax.complex(values[..., :width], values[..., width:])


def from_complex(values):
    return jnp.concatenate([jnp.real(values), jnp.imag(values)], axis=-1)


def sample_blocks(tiles, tile_index, kernel_cols, kernel_rows):
    picked = jnp.take(tiles, tile_index, axis=0)
    col_weight = kernel_cols.astype(jnp.float32).reshape(NBLK, SB, TX)
    row_weight = kernel_rows.astype(jnp.float32).reshape(NBLK, SB, TY)
    partial_sum = jnp.einsum("bcyx,bsx->bcys", picked, col_weight, precision=highest)
    return jnp.einsum("bcys,bsy->bcs", partial_sum, row_weight, precision=highest)


def spread_blocks(values, kernel_cols, kernel_rows):
    col_weight = kernel_cols.astype(jnp.float32).reshape(NBLK, SB, TX)
    row_weight = kernel_rows.astype(jnp.float32).reshape(NBLK, SB, TY)
    partial_sum = jnp.einsum("bcs,bsy->bcys", values, row_weight, precision=highest)
    return jnp.einsum("bcys,bsx->bcyx", partial_sum, col_weight, precision=highest)


def forward_slice(image, profiles, phase_cos, phase_sin, tile_index, kernel_cols, kernel_rows):
    coils = coil_images(profiles, image)
    grid = from_complex(jnp.fft.fft2(to_complex(coils), norm="ortho"))
    predicted = sample_blocks(to_tiles(grid), tile_index, kernel_cols, kernel_rows)
    predicted = predicted.reshape(NBLK, COILS, 2, SB)
    real_part, imag_part = predicted[:, :, 0], predicted[:, :, 1]
    cosine, sine = phase_cos[:, None, None], phase_sin[:, None, None]
    turned = jnp.stack([cosine * real_part - sine * imag_part, sine * real_part + cosine * imag_part], axis=2)
    return turned.transpose(1, 2, 0, 3).reshape(COILS, 2, SAMPLES)


def adjoint_slice(kspace, profiles, phase_cos, phase_sin, tile_index, kernel_cols, kernel_rows):
    shaped = kspace.reshape(COILS, 2, NBLK, SB)
    real_part, imag_part = shaped[:, 0], shaped[:, 1]
    cosine, sine = phase_cos[None, :, None], phase_sin[None, :, None]
    back = jnp.stack([cosine * real_part + sine * imag_part, cosine * imag_part - sine * real_part], axis=1)
    values = back.transpose(2, 0, 1, 3).reshape(NBLK, COILS * 2, SB)
    spread = spread_blocks(values, kernel_cols, kernel_rows)
    summed = jax.ops.segment_sum(spread, tile_index, num_segments=NTILES)
    grid = from_tiles(summed, COILS)
    image = from_complex(jnp.fft.ifft2(to_complex(grid), norm="ortho"))
    return combine_coils(profiles, image)


def phases(caipi_cycle):
    blocks = jnp.arange(NBLK, dtype=jnp.int32)
    turns = (caipi_cycle[:, None] * blocks[None, :]) % MB
    angle = turns.astype(jnp.float32) * (two_pi / MB)
    return jnp.cos(angle), jnp.sin(angle)


def edge_term(values, weights, axis):
    count = values.shape[axis]
    diff = lax.slice_in_dim(values, 0, count - 1, axis=axis) - lax.slice_in_dim(values, 1, count, axis=axis)
    coupling = lax.slice_in_dim(weights, 0, count - 1, axis=axis) * lax.slice_in_dim(weights, 1, count, axis=axis)
    flux = coupling * diff
    after = [(0, 0)] * values.ndim
    before = [(0, 0)] * values.ndim
    after[axis] = (0, 1)
    before[axis] = (1, 0)
    return jnp.pad(flux, after) - jnp.pad(flux, before)


def laplace(images, weights):
    doubled = jnp.concatenate([weights, weights], axis=-1)
    total = edge_term(images, doubled, 1) + edge_term(images, doubled, 2)
    shaped = images.reshape(images.shape[:-1] + (2, NX))
    columns = edge_term(shaped, weights[..., None, :], shaped.ndim - 1)
    return total + columns.reshape(images.shape)


def reference(kspace_data, coil_maps, smooth_weight, kernel_cols, kernel_rows, tile_index, caipi_cycle):
    phase_cos, phase_sin = phases(caipi_cycle)
    flat_cos = jnp.repeat(phase_cos, GROUPS, axis=0)
    flat_sin = jnp.repeat(phase_sin, GROUPS, axis=0)
    flat_maps = coil_maps.reshape(MB * GROUPS, COILS, NY, 2 * NX)

    def forward_one(inputs):
        image, profiles, cosine, sine = inputs
        return forward_slice(image, profiles, cosine, sine, tile_index, kernel_cols, kernel_rows)

    def adjoint_one(inputs):
        kspace, profiles, cosine, sine = inputs
        return adjoint_slice(kspace, profiles, cosine, sine, tile_index, kernel_cols, kernel_rows)

    def forward_all(images):
        flat_images = images.reshape(MB * GROUPS, NY, 2 * NX)
        predicted = lax.map(forward_one, (flat_images, flat_maps, flat_cos, flat_sin))
        return jnp.sum(predicted.reshape(MB, GROUPS, COILS, 2, SAMPLES), axis=0)

    def adjoint_all(collapsed):
        spread = jnp.broadcast_to(collapsed[None], (MB,) + collapsed.shape).reshape(MB * GROUPS, COILS, 2, SAMPLES)
        images = lax.map(adjoint_one, (spread, flat_maps, flat_cos, flat_sin))
        return images.reshape(MB, GROUPS, NY, 2 * NX)

    def apply_normal(direction):
        return adjoint_all(forward_all(direction)) + reg_strength * laplace(direction, smooth_weight) + damping * direction

    rhs = adjoint_all(kspace_data)
    solution_field = jnp.zeros_like(rhs)
    residual = rhs
    direction = rhs
    norm_now = jnp.sum(residual * residual)
    for step in range(ITERS):
        image = apply_normal(direction)
        alpha = norm_now / jnp.sum(direction * image)
        solution_field = solution_field + alpha * direction
        residual = residual - alpha * image
        norm_next = jnp.sum(residual * residual)
        direction = residual + (norm_next / norm_now) * direction
        norm_now = norm_next
    return solution_field, residual
```

```python
import functools
import math

import jax
import jax.numpy as jnp
from jax import lax
from jax.experimental import pallas as pl
from jax.experimental.pallas import tpu as pltpu
from jax.sharding import PartitionSpec as P

NY = 256
NX = 256
TY = 16
TX = 16
SB = 128
NBLK = 16
HALF = NX // 2

reg_strength = 0.5
damping = 1.0
f32 = jnp.float32
bf16 = jnp.bfloat16
MESH = pl.DeviceIdType.MESH


def cos_turn(n):
    n = n - 256.0 * jnp.floor(n * (1.0 / 256.0))
    t = (jnp.abs(n - 128.0) - 64.0) * (2.0 * math.pi / 256.0)
    u = t * t
    series = -1.0 / math.factorial(11)
    for order, sign in ((9, 1.0), (7, -1.0), (5, 1.0), (3, -1.0), (1, 1.0)):
        series = sign / math.factorial(order) + u * series
    return t * series


def sin_turn(n):
    return cos_turn(n + 192.0)


def split(x):
    high = x.astype(bf16)
    return high, (x - high.astype(f32)).astype(bf16)


def mm(a, b):
    return jnp.dot(a, b, preferred_element_type=f32)


def mm_nt(a, b):
    return lax.dot_general(a, b, (((1,), (1,)), ((), ())), preferred_element_type=f32)


def iota(shape, axis):
    return lax.broadcasted_iota(jnp.int32, shape, axis)


def kernel(
    dims,
    coil_hbm,
    ks_ref,
    w_ref,
    kc_ref,
    kr_ref,
    tile_ref,
    caipi_ref,
    x_ref,
    res_ref,
    coil_v,
    coil_send,
    coil_buf,
    ks_part,
    row_p,
    row_k,
    col_q,
    col_f,
    kc2,
    kr2,
    mask_ref,
    y_ref,
    v_ref,
    v_tot,
    pair_in,
    own_sum,
    band_in,
    own_tot,
    part1,
    part2,
    rs1,
    rs2,
    gsum,
    rg,
    vext,
    vgrp,
    wext,
    wgrp,
    lap_ref,
    sc_out,
    sc_in,
    ssem,
    rsem,
    lsem,
):
    nb, ny, nz, nr = dims
    ng = ny * nz
    rb = NY // nr
    b = lax.axis_index("band")
    g = lax.axis_index("grp")
    r = lax.axis_index("row")
    h = lax.rem(r, 2)
    partner = {"row": r + 1 - 2 * h}
    gy = lax.div(g, nz)
    gz = lax.rem(g, nz)
    row_peer = [{"row": lax.rem(r + o, nr)} for o in range(1, nr)]
    band_peer = [{"band": lax.rem(b + o, nb)} for o in range(1, nb)]
    y_peer = [{"grp": lax.rem(gy + o, ny) * nz + gz} for o in range(1, ny)]
    z_peer = [
        {"grp": gy * nz + gz + 1 - 2 * lax.rem(gz, 2)},
        {"grp": gy * nz + nz - 1 - gz},
    ]
    g_next = {"grp": lax.rem(g + 1, ng)}
    g_prev = {"grp": lax.rem(g + ng - 1, ng)}
    peers = row_peer + band_peer + y_peer + z_peer + [g_next, g_prev]

    barrier = pltpu.get_barrier_semaphore()
    for peer in peers:
        pl.semaphore_signal(barrier, inc=1, device_id=peer, device_id_type=MESH)

    coil_copy = pltpu.make_async_copy(coil_hbm, coil_v, lsem)
    coil_copy.start()

    slots = iter(range(128))
    started = []

    def send(src, dst, peer):
        slot = next(slots)
        copy = pltpu.make_async_remote_copy(
            src_ref=src,
            dst_ref=dst,
            send_sem=ssem.at[slot],
            recv_sem=rsem.at[slot],
            device_id=peer,
            device_id_type=MESH,
        )
        copy.start()
        started.append(copy)
        return copy

    lane = iota((1, 256), 1)
    lane_block = lax.shift_right_logical(lane, 4)
    lane_f = jnp.zeros((1, 256), f32)
    lane_m = jnp.zeros((1, 256), f32)
    lane_c = jnp.zeros((1, 256), f32)
    within = jnp.bitwise_and(lane, 15).astype(f32)
    q_half = (iota((16, HALF), 1) + h * HALF).astype(f32)
    p_lane = iota((16, 256), 1).astype(f32)
    sub16_q = iota((16, HALF), 0).astype(f32)
    sub16 = iota((16, 256), 0).astype(f32)
    scale = 1.0 / 16.0
    cycle = caipi_ref[0]
    for k in range(NBLK):
        tile = tile_ref[k]
        ty = jnp.right_shift(tile, 4).astype(f32) * 16.0
        tx = jnp.bitwise_and(tile, 15).astype(f32) * 16.0
        back = 256.0 - 64.0 * jnp.bitwise_and(cycle * k, 3).astype(f32)
        lane_f = jnp.where(lane_block == k, ty, lane_f)
        lane_m = jnp.where(lane_block == k, back, lane_m)
        lane_c = jnp.where(lane_block == k, tx, lane_c)
        rows = slice(k * 16, k * 16 + 16)
        turn = p_lane * (sub16 + ty) + back
        for part, values in ((0, cos_turn(turn)), (1, sin_turn(turn))):
            high, low = split(values * scale)
            row_k[0, part * 256 + k * 16 : part * 256 + k * 16 + 16, :] = high
            row_k[1, part * 256 + k * 16 : part * 256 + k * 16 + 16, :] = low
        turn = q_half * (sub16_q + tx)
        for part, values in ((0, cos_turn(turn)), (1, sin_turn(turn))):
            high, low = split(values * scale)
            col_q[0, rows, part * HALF : part * HALF + HALF] = high
            col_q[1, rows, part * HALF : part * HALF + HALF] = low
        kc2[rows, :] = kc_ref[:, k * SB : k * SB + SB]
        kr2[rows, :] = kr_ref[:, k * SB : k * SB + SB].astype(f32)
    lane_f = lane_f + within
    lane_c = lane_c + within
    turn = iota((256, 256), 0).astype(f32) * lane_f + lane_m
    for part, values in ((0, cos_turn(turn)), (1, sin_turn(turn))):
        high, low = split(values * scale)
        row_p[0, part * 256 : part * 256 + 256, :] = high
        row_p[1, part * 256 : part * 256 + 256, :] = low
    turn = (iota((HALF, 256), 0) + h * HALF).astype(f32) * lane_c
    cosine, sine = cos_turn(turn) * scale, sin_turn(turn) * scale
    for level, (cos_part, sin_part) in enumerate(zip(split(cosine), split(sine))):
        col_f[level, :HALF, :256] = cos_part
        col_f[level, :HALF, 256:] = -sin_part
        col_f[level, HALF:, :256] = sin_part
        col_f[level, HALF:, 256:] = cos_part
    mask_ref[...] = (
        lax.shift_right_logical(iota((256, 256), 0), 4)
        == lax.shift_right_logical(iota((256, 256), 1), 4)
    ).astype(f32)

    pl.semaphore_wait(barrier, len(peers))

    ks_copy = send(ks_ref, ks_part, partner)
    coil_copy.wait()

    def half_of(part, half):
        return pl.ds(pl.multiple_of(part * NX + half * HALF, HALF), HALF)

    for c in range(2):
        for part in range(2):
            to = slice(part * HALF, part * HALF + HALF)
            coil_send[c, :, to] = coil_v[c, :, half_of(part, 1 - h)].astype(f32)
            coil_buf[c, :, to] = coil_v[c, :, half_of(part, h)].astype(f32)
    partner_coils = send(coil_send, coil_buf.at[pl.ds(2, 2)], partner)
    w_copies = [
        send(w_ref, wgrp.at[0], g_next),
        send(w_ref, wgrp.at[1], g_prev),
        send(w_ref.at[pl.ds(rb - 8, 8)], wext.at[pl.ds(0, 8)], {"row": lax.rem(r + 1, nr)}),
        send(w_ref.at[pl.ds(0, 8)], wext.at[pl.ds(rb + 8, 8)], {"row": lax.rem(r + nr - 1, nr)}),
    ]
    wext[8 : 8 + rb, :] = w_ref[...]

    def back_project(values, c, out, first):
        for ch in range(2):
            for k in range(NBLK):
                row = (c * 2 + ch) * NBLK + k
                weighted = kr2[k * 16 : k * 16 + 16, :] * values[row : row + 1, :]
                high, low = split(weighted)
                at = (ch * NBLK + k) * 16
                y_ref[0, at : at + 16, :] = high
                y_ref[1, at : at + 16, :] = low
        tiles = mm_nt(y_ref[0], kc2[...]) + mm_nt(y_ref[1], kc2[...])
        keep = mask_ref[...]
        high_r, low_r = split(tiles[:256] * keep)
        high_i, low_i = split(tiles[256:] * keep)
        q_high, q_low = col_q[0], col_q[1]
        a_r = mm(high_r, q_high) + (mm(high_r, q_low) + mm(low_r, q_high))
        a_i = mm(high_i, q_high) + (mm(high_i, q_low) + mm(low_i, q_high))
        u = jnp.concatenate(
            [a_r[:, :HALF] - a_i[:, HALF:], a_r[:, HALF:] + a_i[:, :HALF]], axis=1
        )
        high, low = split(u)
        p_high, p_low = row_p[0], row_p[1]
        mixed = mm(p_high, high) + (mm(p_high, low) + mm(p_low, high))
        im_r = mixed[:256, :HALF] - mixed[256:, HALF:]
        im_i = mixed[:256, HALF:] + mixed[256:, :HALF]
        coil_r, coil_i = coil_buf[c, :, :HALF], coil_buf[c, :, HALF:]
        sum_r = coil_r * im_r + coil_i * im_i
        sum_i = coil_r * im_i - coil_i * im_r
        if first:
            out[:, :HALF] = sum_r
            out[:, HALF:] = sum_i
        else:
            out[:, :HALF] += sum_r
            out[:, HALF:] += sum_i

    def scatter(part, slots_in):
        return [
            send(
                part.at[pl.ds(pl.multiple_of(row_peer[o - 1]["row"] * rb, rb), rb)],
                slots_in.at[o],
                row_peer[o - 1],
            )
            for o in range(1, nr)
        ]

    my_rows = pl.ds(pl.multiple_of(r * rb, rb), rb)

    def collect(part, slots_in, copies):
        same = part[my_rows, :]
        for o in range(2, nr, 2):
            copies[o - 1].wait_recv()
            same = same + slots_in[o]
        copies[0].wait_recv()
        diff = slots_in[1]
        for o in range(3, nr, 2):
            copies[o - 1].wait_recv()
            diff = diff + slots_in[o]
        return same, diff

    def widen(same, diff):
        even = h == 0
        return (
            jnp.where(even, same[:, :HALF], diff[:, :HALF]),
            jnp.where(even, diff[:, :HALF], same[:, :HALF]),
            jnp.where(even, same[:, HALF:], diff[:, HALF:]),
            jnp.where(even, diff[:, HALF:], same[:, HALF:]),
        )

    for c in range(2):
        for ch in range(2):
            for k in range(NBLK):
                row = (c * 2 + ch) * NBLK + k
                v_ref[row : row + 1, :] = ks_ref[c, ch : ch + 1, k * SB : k * SB + SB]
    back_project(v_ref, 0, part1, True)
    back_project(v_ref, 1, part1, False)
    ks_copy.wait_recv()
    for c in range(2):
        for ch in range(2):
            for k in range(NBLK):
                row = ((c + 2) * 2 + ch) * NBLK + k
                v_ref[row : row + 1, :] = ks_part[c, ch : ch + 1, k * SB : k * SB + SB]
    partner_coils.wait_recv()
    back_project(v_ref, 2, part1, False)
    back_project(v_ref, 3, part1, False)
    copies = scatter(part1, rs1)
    same, diff = collect(part1, rs1, copies)
    gsum[0] = same
    gsum[1] = diff
    gathered = [
        send(gsum.at[o % 2], rg.at[my_rows], row_peer[o - 1]) for o in range(1, nr)
    ]
    rg[my_rows, :] = same
    for at, piece in enumerate(widen(same, diff)):
        vext[8 : 8 + rb, at * HALF : at * HALF + HALF] = piece
    v_copies = [
        send(vext.at[pl.ds(rb, 8)], vext.at[pl.ds(0, 8)], {"row": lax.rem(r + 1, nr)}),
        send(vext.at[pl.ds(8, 8)], vext.at[pl.ds(rb + 8, 8)], {"row": lax.rem(r + nr - 1, nr)}),
        send(vext.at[pl.ds(8, rb)], vgrp.at[0], g_next),
        send(vext.at[pl.ds(8, rb)], vgrp.at[1], g_prev),
    ]
    for copy in gathered:
        copy.wait_recv()

    weights = jnp.concatenate([kr2[...], kr2[...]], axis=0)
    for c in (2, 3, 0, 1):
        coil_r, coil_i = coil_buf[c, :, :HALF], coil_buf[c, :, HALF:]
        image_r, image_i = rg[:, :HALF], rg[:, HALF:]
        high, low = split(
            jnp.concatenate(
                [coil_r * image_r - coil_i * image_i, coil_r * image_i + coil_i * image_r],
                axis=1,
            )
        )
        k_high, k_low = row_k[0], row_k[1]
        mixed = mm(k_high, high) + (mm(k_high, low) + mm(k_low, high))
        high, low = split(
            jnp.concatenate(
                [
                    mixed[:256, :HALF] + mixed[256:, HALF:],
                    mixed[:256, HALF:] - mixed[256:, :HALF],
                ],
                axis=1,
            )
        )
        f_high, f_low = col_f[0], col_f[1]
        grid = mm(high, f_high) + (mm(high, f_low) + mm(low, f_high))
        keep = mask_ref[...]
        high, low = split(
            jnp.concatenate([grid[:, :256] * keep, grid[:, 256:] * keep], axis=0)
        )
        sampled = (mm(high, kc2[...]) + mm(low, kc2[...])) * weights
        v_ref[c * 32 : c * 32 + 32, :] = jnp.sum(sampled.reshape(32, 16, SB), axis=1)
        if c == 3:
            pair = send(v_ref.at[pl.ds(64, 64)], pair_in, partner)
    pair.wait_recv()
    own_sum[...] = v_ref[0:64, :] + pair_in[...]
    bands = [send(own_sum, band_in.at[o], band_peer[o - 1]) for o in range(1, nb)]

    for copy in w_copies + v_copies:
        copy.wait_recv()
    w = w_ref[...]
    row_at = iota((rb, NX), 0)
    col_at = iota((rb, NX), 1)
    zero = jnp.zeros((rb, NX), f32)
    w_up = jnp.where((row_at == 0) & (r == 0), zero, wext[7 : 7 + rb, :])
    w_down = jnp.where((row_at == rb - 1) & (r == nr - 1), zero, wext[9 : 9 + rb, :])
    w_left = jnp.where(col_at == 0, zero, pltpu.roll(w, 1, 1))
    w_right = jnp.where(col_at == NX - 1, zero, pltpu.roll(w, NX - 1, 1))
    w_prev = jnp.where(g == 0, zero, wgrp[0])
    w_next = jnp.where(g == ng - 1, zero, wgrp[1])
    power = jnp.zeros((1, SB), f32)
    energy = jnp.zeros((1, SB), f32)
    for ch in range(2):
        cols = slice(ch * NX, ch * NX + NX)
        v = vext[8 : 8 + rb, cols]
        total = w_up * (v - vext[7 : 7 + rb, cols])
        total += w_down * (v - vext[9 : 9 + rb, cols])
        total += w_left * (v - pltpu.roll(v, 1, 1))
        total += w_right * (v - pltpu.roll(v, NX - 1, 1))
        total += w_prev * (v - vgrp[0, :, cols])
        total += w_next * (v - vgrp[1, :, cols])
        smoothed = reg_strength * (w * total) + damping * v
        lap_ref[:, cols] = smoothed
        squares = jnp.sum(v * v, axis=0, keepdims=True)
        power = power + squares[:, :SB] + squares[:, SB:]
        squares = jnp.sum(v * smoothed, axis=0, keepdims=True)
        energy = energy + squares[:, :SB] + squares[:, SB:]

    tot = own_sum[...]
    for o in range(1, nb):
        bands[o - 1].wait_recv()
        tot = tot + band_in[o]
    own_tot[...] = tot
    back = send(own_tot, v_tot.at[pl.ds(64, 64)], partner)
    v_tot[0:64, :] = tot
    energy = energy + jnp.sum(tot * tot, axis=0, keepdims=True) * (1.0 / nb)

    row8 = iota((8, SB), 0)
    tile_sum = jnp.where(row8 == 0, power, jnp.where(row8 == 1, energy, 0.0))
    count = iter(range(32))

    def stage_start(index, value, stage_peers):
        sc_out[index] = value
        return [(at, send(sc_out.at[index], sc_in.at[at], peer)) for at, peer in zip(count, stage_peers)]

    def stage_end(value, copies):
        for at, copy in copies:
            copy.wait_recv()
            value = value + sc_in[at]
        return value

    first = stage_start(0, tile_sum, row_peer)

    back_project(v_tot, 0, part2, True)
    back_project(v_tot, 1, part2, False)
    back.wait_recv()
    tile_sum = stage_end(tile_sum, first)
    second = stage_start(1, tile_sum, band_peer)
    back_project(v_tot, 2, part2, False)
    back_project(v_tot, 3, part2, False)
    copies = scatter(part2, rs2)
    tile_sum = stage_end(tile_sum, second)
    tile_sum = stage_end(tile_sum, stage_start(2, tile_sum, y_peer))
    tile_sum = stage_end(tile_sum, stage_start(3, tile_sum, z_peer[:1]))
    tile_sum = stage_end(tile_sum, stage_start(4, tile_sum, z_peer[1:]))
    totals = jnp.sum(tile_sum, axis=1, keepdims=True)
    alpha = totals[0:1] / totals[1:2]
    same, diff = collect(part2, rs2, copies)
    for at, piece in enumerate(widen(same, diff)):
        cols = slice(at * HALF, at * HALF + HALF)
        v = vext[8 : 8 + rb, cols]
        x_ref[:, cols] = alpha * v
        res_ref[:, cols] = v - alpha * (piece + lap_ref[:, cols])
    for copy in started:
        copy.wait_send()


def on_device(
    dims, kspace_data, coil_maps, smooth_weight, kernel_cols, kernel_rows, tile_index, caipi_cycle
):
    nb, ny, nz, nr = dims
    rb = NY // nr
    vmem = pl.BlockSpec(memory_space=pltpu.VMEM)
    smem = pl.BlockSpec(memory_space=pltpu.SMEM)
    field = jax.ShapeDtypeStruct((rb, 2 * NX), f32)
    solution_field, residual = pl.pallas_call(
        functools.partial(kernel, dims),
        out_shape=(field, field),
        in_specs=[pl.BlockSpec(memory_space=pl.ANY), vmem, vmem, vmem, vmem, smem, smem],
        out_specs=(vmem, vmem),
        scratch_shapes=[
            pltpu.VMEM((2, NY, 2 * NX), bf16),
            pltpu.VMEM((2, NY, NX), f32),
            pltpu.VMEM((4, NY, NX), f32),
            pltpu.VMEM((2, 2, NBLK * SB), f32),
            pltpu.VMEM((2, 512, 256), bf16),
            pltpu.VMEM((2, 512, 256), bf16),
            pltpu.VMEM((2, 256, 256), bf16),
            pltpu.VMEM((2, 256, 512), bf16),
            pltpu.VMEM((256, SB), bf16),
            pltpu.VMEM((256, SB), f32),
            pltpu.VMEM((256, 256), f32),
            pltpu.VMEM((2, 512, SB), bf16),
            pltpu.VMEM((128, SB), f32),
            pltpu.VMEM((128, SB), f32),
            pltpu.VMEM((64, SB), f32),
            pltpu.VMEM((64, SB), f32),
            pltpu.VMEM((nb, 64, SB), f32),
            pltpu.VMEM((64, SB), f32),
            pltpu.VMEM((NY, NX), f32),
            pltpu.VMEM((NY, NX), f32),
            pltpu.VMEM((nr, rb, NX), f32),
            pltpu.VMEM((nr, rb, NX), f32),
            pltpu.VMEM((2, rb, NX), f32),
            pltpu.VMEM((NY, NX), f32),
            pltpu.VMEM((rb + 16, 2 * NX), f32),
            pltpu.VMEM((2, rb, 2 * NX), f32),
            pltpu.VMEM((rb + 16, NX), f32),
            pltpu.VMEM((2, rb, NX), f32),
            pltpu.VMEM((rb, 2 * NX), f32),
            pltpu.VMEM((5, 8, SB), f32),
            pltpu.VMEM((32, 8, SB), f32),
            pltpu.SemaphoreType.DMA((64,)),
            pltpu.SemaphoreType.DMA((64,)),
            pltpu.SemaphoreType.DMA,
        ],
        compiler_params=pltpu.CompilerParams(
            collective_id=0, has_side_effects=True, vmem_limit_bytes=48 * 1024 * 1024
        ),
    )(
        coil_maps[0, 0],
        kspace_data[0],
        smooth_weight[0, 0],
        kernel_cols.T,
        kernel_rows.T,
        tile_index,
        caipi_cycle,
    )
    return solution_field[None, None], residual[None, None]


def solution(mesh, split_grp=(4, 4)):
    dims = (mesh.shape["band"],) + tuple(split_grp) + (mesh.shape["row"],)
    return jax.shard_map(
        functools.partial(on_device, dims),
        mesh=mesh,
        in_specs=(
            P("grp", "row", None, None),
            P("band", "grp", "row", None, None),
            P("band", "grp", "row", None),
            P(),
            P(),
            P(),
            P("band"),
        ),
        out_specs=(P("band", "grp", "row", None), P("band", "grp", "row", None)),
        check_vma=False,
    )
```

```python
import functools
import math

import jax
import jax.numpy as jnp
from jax import lax
from jax.experimental import pallas as pl
from jax.experimental.pallas import tpu as pltpu
from jax.sharding import PartitionSpec as P

NY = 256
NX = 256
TY = 16
TX = 16
SB = 128
NBLK = 16
HALF = NX // 2

reg_strength = 0.5
damping = 1.0
f32 = jnp.float32
bf16 = jnp.bfloat16
MESH = pl.DeviceIdType.MESH


def cos_turn(n):
    n = n - 256.0 * jnp.floor(n * (1.0 / 256.0))
    t = (jnp.abs(n - 128.0) - 64.0) * (2.0 * math.pi / 256.0)
    u = t * t
    series = -1.0 / math.factorial(11)
    for order, sign in ((9, 1.0), (7, -1.0), (5, 1.0), (3, -1.0), (1, 1.0)):
        series = sign / math.factorial(order) + u * series
    return t * series


def sin_turn(n):
    return cos_turn(n + 192.0)


def split(x):
    high = x.astype(bf16)
    return high, (x - high.astype(f32)).astype(bf16)


def mm(a, b):
    return jnp.dot(a, b, preferred_element_type=f32)


def mm_nt(a, b):
    return lax.dot_general(a, b, (((1,), (1,)), ((), ())), preferred_element_type=f32)


def iota(shape, axis):
    return lax.broadcasted_iota(jnp.int32, shape, axis)


def kernel(
    dims,
    coil_hbm,
    ks_hbm,
    w_hbm,
    kc_hbm,
    kr_hbm,
    tile_ref,
    caipi_ref,
    x_ref,
    res_ref,
    coil_v,
    coil_send,
    coil_buf,
    ks_own,
    ks_part,
    w_ref,
    kc_v,
    kr_v,
    row_p,
    row_k,
    col_q,
    col_f,
    kc_nt,
    kc_nn,
    kr2,
    v_ref,
    v_tot,
    pair_in,
    own_sum,
    band_in,
    own_tot,
    part1,
    part2,
    rs1,
    rs2,
    gsum,
    rg,
    vext,
    vgrp,
    wext,
    wgrp,
    lap_ref,
    sc_out,
    sc_in,
    ssem,
    rsem,
    lsem,
):
    nb, ny, nz, nr = dims
    ng = ny * nz
    nl = nr // 2
    rb = NY // nr
    b = lax.axis_index("band")
    g = lax.axis_index("grp")
    r = lax.axis_index("row")
    h = lax.rem(r, 2)
    zl = lax.div(r, 2)
    gy = lax.div(g, nz)
    gz = lax.rem(g, nz)
    partner = {"row": r + 1 - 2 * h}
    row_peer = [{"row": lax.rem(r + o, nr)} for o in range(1, nr)]
    band_peer = [{"band": lax.rem(b + o, nb)} for o in range(1, nb)]
    plane_peer = [
        {"grp": lax.rem(gy + o, ny) * nz + gz, "row": zl * 2 + lax.rem(h + i, 2)}
        for o in range(ny)
        for i in range(2)
        if o or i
    ]
    line = gz * nl + zl
    line_peer = []
    for o in range(1, nz * nl):
        at = lax.rem(line + o, nz * nl)
        line_peer.append({"grp": gy * nz + lax.div(at, nl), "row": lax.rem(at, nl) * 2 + h})
    g_next = {"grp": lax.rem(g + 1, ng)}
    g_prev = {"grp": lax.rem(g + ng - 1, ng)}
    peers = row_peer + band_peer + plane_peer + line_peer + [g_next, g_prev]

    barrier = pltpu.get_barrier_semaphore()
    for peer in peers:
        pl.semaphore_signal(barrier, inc=1, device_id=peer, device_id_type=MESH)
    fetches = [
        pltpu.make_async_copy(src, dst, lsem.at[at])
        for at, (src, dst) in enumerate(
            ((kc_hbm, kc_v), (kr_hbm, kr_v), (ks_hbm, ks_own), (coil_hbm, coil_v), (w_hbm, w_ref))
        )
    ]
    for copy in fetches:
        copy.start()

    slots = iter(range(128))
    started = []

    def send(src, dst, peer):
        slot = next(slots)
        copy = pltpu.make_async_remote_copy(
            src_ref=src,
            dst_ref=dst,
            send_sem=ssem.at[slot],
            recv_sem=rsem.at[slot],
            device_id=peer,
            device_id_type=MESH,
        )
        copy.start()
        started.append(copy)
        return copy

    lane = iota((1, 256), 1)
    lane_block = lax.shift_right_logical(lane, 4)
    lane_f = jnp.zeros((1, 256), f32)
    lane_m = jnp.zeros((1, 256), f32)
    lane_c = jnp.zeros((1, 256), f32)
    within = jnp.bitwise_and(lane, 15).astype(f32)
    q_half = (iota((16, HALF), 1) + h * HALF).astype(f32)
    p_lane = iota((16, 256), 1).astype(f32)
    sub16_q = iota((16, HALF), 0).astype(f32)
    sub16 = iota((16, 256), 0).astype(f32)
    scale = 1.0 / 16.0
    cycle = caipi_ref[0]
    for k in range(NBLK):
        tile = tile_ref[k]
        ty = jnp.right_shift(tile, 4).astype(f32) * 16.0
        tx = jnp.bitwise_and(tile, 15).astype(f32) * 16.0
        turns = 256.0 - 64.0 * jnp.bitwise_and(cycle * k, 3).astype(f32)
        lane_f = jnp.where(lane_block == k, ty, lane_f)
        lane_m = jnp.where(lane_block == k, turns, lane_m)
        lane_c = jnp.where(lane_block == k, tx, lane_c)
        turn = p_lane * (sub16 + ty) + turns
        for part, values in ((0, cos_turn(turn)), (1, sin_turn(turn))):
            high, low = split(values * scale)
            at = part * 256 + k * 16
            row_k[at : at + 16, 0:256] = high
            row_k[at : at + 16, 256:512] = high
            row_k[at : at + 16, 512:768] = low
        turn = q_half * (sub16_q + tx)
        half, at = k // 8, (k % 8) * 16
        for part, values in ((0, cos_turn(turn)), (1, sin_turn(turn))):
            high, low = split(values * scale)
            to = slice(part * HALF, part * HALF + HALF)
            col_q[half, at : at + 16, to] = high
            col_q[half, 128 + at : 128 + at + 16, to] = low
            col_q[half, 256 + at : 256 + at + 16, to] = high
    lane_f = lane_f + within
    lane_c = lane_c + within
    turn = iota((256, 256), 0).astype(f32) * lane_f + lane_m
    for part, values in ((0, cos_turn(turn)), (1, sin_turn(turn))):
        high, low = split(values * scale)
        row_p[part, :, 0:256] = high
        row_p[part, :, 256:512] = high
        row_p[part, :, 512:768] = low
    turn = (iota((HALF, 256), 0) + h * HALF).astype(f32) * lane_c
    cosine, sine = cos_turn(turn) * scale, sin_turn(turn) * scale
    levels = tuple(zip(split(cosine), split(sine)))
    for third, level in enumerate((0, 1, 0)):
        cos_part, sin_part = levels[level]
        at = third * 256
        for half in range(2):
            cols = slice(half * 128, half * 128 + 128)
            col_f[half, at : at + 128, 0:128] = cos_part[:, cols]
            col_f[half, at : at + 128, 128:256] = -sin_part[:, cols]
            col_f[half, at + 128 : at + 256, 0:128] = sin_part[:, cols]
            col_f[half, at + 128 : at + 256, 128:256] = cos_part[:, cols]
    fetches[0].wait()
    fetches[1].wait()
    for k in range(NBLK):
        half, at = k // 8, (k % 8) * 16
        cols = slice(k * SB, k * SB + SB)
        piece = kc_v[:, cols]
        kc_nt[half, at : at + 16, 0:SB] = piece
        kc_nt[half, at : at + 16, SB : 2 * SB] = piece
        kc_nn[half, at : at + 16, :] = piece
        kc_nn[half, 128 + at : 128 + at + 16, :] = piece
        kr2[k * 16 : k * 16 + 16, :] = kr_v[:, cols].astype(f32)
    keep = (
        lax.shift_right_logical(iota((128, 128), 0), 4)
        == lax.shift_right_logical(iota((128, 128), 1), 4)
    )
    keep2 = jnp.concatenate([keep, keep], axis=0)

    def spread(row_of, c):
        blocks = []
        for half in range(2):
            pieces = []
            for ch in range(2):
                for k in range(half * 8, half * 8 + 8):
                    pieces.append(kr2[k * 16 : k * 16 + 16, :] * row_of(c, ch, k))
            high, low = split(jnp.concatenate(pieces, axis=0))
            tiles = mm_nt(jnp.concatenate([high, low], axis=1), kc_nt[half])
            high, low = split(jnp.where(keep2, tiles, 0.0))
            mixed = mm(jnp.concatenate([high, high, low], axis=1), col_q[half])
            blocks.append(
                jnp.concatenate(
                    [
                        mixed[:128, :HALF] - mixed[128:, HALF:],
                        mixed[:128, HALF:] + mixed[128:, :HALF],
                    ],
                    axis=1,
                )
            )
        high, low = split(jnp.concatenate(blocks, axis=0))
        return jnp.concatenate([high, low, high], axis=0)

    far = pl.multiple_of(jnp.where(zl >= nl // 2, 0, 128), 128)
    near = pl.multiple_of(128 - far, 128)

    def row_stage(factors, coils, start):
        rows = pl.ds(start, 128)
        left = jnp.concatenate([row_p[0, rows, :], row_p[1, rows, :]], axis=0)
        sum_r = sum_i = None
        for factor, c in zip(factors, coils):
            mixed = mm(left, factor)
            im_r = mixed[:128, :HALF] - mixed[128:, HALF:]
            im_i = mixed[:128, HALF:] + mixed[128:, :HALF]
            coil_r, coil_i = coil_buf[c, rows, :HALF], coil_buf[c, rows, HALF:]
            term_r = coil_r * im_r + coil_i * im_i
            term_i = coil_r * im_i - coil_i * im_r
            sum_r = term_r if sum_r is None else sum_r + term_r
            sum_i = term_i if sum_i is None else sum_i + term_i
        return jnp.concatenate([sum_r, sum_i], axis=1)

    def from_ref(ref):
        return lambda c, ch, k: ref[(c * 2 + ch) * NBLK + k : (c * 2 + ch) * NBLK + k + 1, :]

    def from_samples(ref, base):
        return lambda c, ch, k: ref[c - base, ch : ch + 1, k * SB : k * SB + SB]

    nq = 128 // rb
    inner = lax.rem(r, nq)
    near_base = lax.div(r, nq) * nq
    far_base = nq - near_base
    targets = [(True, i) for i in range(nq)] + [(False, i) for i in range(1, nq)]
    slot_of = {target: at + 1 for at, target in enumerate(targets)}

    def block_of(target):
        return (far_base if target[0] else near_base) + lax.rem(inner + target[1], nq)

    def scatter(part, slots_in, is_far):
        sent = {}
        for target in targets:
            if target[0] == is_far:
                to = block_of(target)
                sent[target] = send(
                    part.at[pl.ds(pl.multiple_of(to * rb, rb), rb)],
                    slots_in.at[slot_of[target]],
                    {"row": to},
                )
        return sent

    def collect(part, slots_in, sent):
        same, diff = part[my_rows, :], None
        for target in [t for t in targets if not t[0]] + [t for t in targets if t[0]]:
            sent[target].wait_recv()
            piece = slots_in[slot_of[target]]
            if target[1] % 2 == 0:
                same = same + piece
            else:
                diff = piece if diff is None else diff + piece
        return same, diff

    def widen(same, diff):
        even = h == 0
        return (
            jnp.where(even, same[:, :HALF], diff[:, :HALF]),
            jnp.where(even, diff[:, :HALF], same[:, :HALF]),
            jnp.where(even, same[:, HALF:], diff[:, HALF:]),
            jnp.where(even, diff[:, HALF:], same[:, HALF:]),
        )

    my_rows = pl.ds(pl.multiple_of(r * rb, rb), rb)

    fetches[2].wait()
    u0 = spread(from_samples(ks_own, 0), 0)
    fetches[3].wait()

    def half_of(part, half):
        return pl.ds(pl.multiple_of(part * NX + half * HALF, HALF), HALF)

    for c in range(2):
        for part in range(2):
            to = slice(part * HALF, part * HALF + HALF)
            coil_send[c, :, to] = coil_v[c, :, half_of(part, 1 - h)].astype(f32)
            coil_buf[c, :, to] = coil_v[c, :, half_of(part, h)].astype(f32)
    fetches[4].wait()
    wext[8 : 8 + rb, :] = w_ref[...]

    pl.semaphore_wait(barrier, len(peers))

    ks_copy = send(ks_own, ks_part, partner)
    partner_coils = send(coil_send, coil_buf.at[pl.ds(2, 2)], partner)
    w_copies = [
        send(w_ref, wgrp.at[0], g_next),
        send(w_ref, wgrp.at[1], g_prev),
        send(w_ref.at[pl.ds(rb - 8, 8)], wext.at[pl.ds(0, 8)], {"row": lax.rem(r + 1, nr)}),
        send(w_ref.at[pl.ds(0, 8)], wext.at[pl.ds(rb + 8, 8)], {"row": lax.rem(r + nr - 1, nr)}),
    ]
    factors = [u0, spread(from_samples(ks_own, 0), 1)]
    ks_copy.wait_recv()
    factors += [spread(from_samples(ks_part, 2), 2), spread(from_samples(ks_part, 2), 3)]
    partner_coils.wait_recv()
    part1[pl.ds(far, 128), :] = row_stage(factors, range(4), far)
    sent = scatter(part1, rs1, True)
    part1[pl.ds(near, 128), :] = row_stage(factors, range(4), near)
    sent.update(scatter(part1, rs1, False))
    same, diff = collect(part1, rs1, sent)
    gsum[0] = same
    gsum[1] = diff
    gathered = [send(gsum.at[t[1] % 2], rg.at[my_rows], {"row": block_of(t)}) for t in targets]
    rg[my_rows, :] = same
    for at, piece in enumerate(widen(same, diff)):
        vext[8 : 8 + rb, at * HALF : at * HALF + HALF] = piece
    v_copies = [
        send(vext.at[pl.ds(rb, 8)], vext.at[pl.ds(0, 8)], {"row": lax.rem(r + 1, nr)}),
        send(vext.at[pl.ds(8, 8)], vext.at[pl.ds(rb + 8, 8)], {"row": lax.rem(r + nr - 1, nr)}),
    ]
    for copy in gathered:
        copy.wait_recv()
    hb = rb // 2
    v_copies += [
        send(vext.at[pl.ds(8, hb)], vgrp.at[1, pl.ds(0, hb)], g_prev),
        send(vext.at[pl.ds(8 + hb, hb)], vgrp.at[0, pl.ds(hb, hb)], g_next),
    ]
    late_copies = [
        send(vext.at[pl.ds(8 + hb, hb)], vgrp.at[1, pl.ds(hb, hb)], g_prev),
        send(vext.at[pl.ds(8, hb)], vgrp.at[0, pl.ds(0, hb)], g_next),
    ]

    for c in (2, 3, 0, 1):
        coil_r, coil_i = coil_buf[c, :, :HALF], coil_buf[c, :, HALF:]
        image_r, image_i = rg[:, :HALF], rg[:, HALF:]
        high, low = split(
            jnp.concatenate(
                [coil_r * image_r - coil_i * image_i, coil_r * image_i + coil_i * image_r],
                axis=1,
            )
        )
        mixed = mm(row_k[...], jnp.concatenate([high, low, high], axis=0))
        high, low = split(
            jnp.concatenate(
                [
                    mixed[:256, :HALF] + mixed[256:, HALF:],
                    mixed[:256, HALF:] - mixed[256:, :HALF],
                ],
                axis=1,
            )
        )
        left = jnp.concatenate([high, high, low], axis=1)
        for half in range(2):
            grid = mm(left[half * 128 : half * 128 + 128], col_f[half])
            grid = jnp.concatenate([grid[:, :128], grid[:, 128:]], axis=0)
            high, low = split(jnp.where(keep2, grid, 0.0))
            sampled = mm(jnp.concatenate([high, low], axis=1), kc_nn[half])
            weights = kr2[half * 128 : half * 128 + 128, :]
            for ch in range(2):
                weighted = sampled[ch * 128 : ch * 128 + 128] * weights
                at = (c * 2 + ch) * NBLK + half * 8
                v_ref[at : at + 8, :] = jnp.sum(weighted.reshape(8, 16, SB), axis=1)
        if c == 3:
            pair = send(v_ref.at[pl.ds(64, 64)], pair_in, partner)
    pair.wait_recv()
    own_sum[...] = v_ref[0:64, :] + pair_in[...]
    bands = [send(own_sum, band_in.at[o], band_peer[o - 1]) for o in range(1, nb)]

    count = iter(range(64))

    def stage_start(index, value, stage_peers):
        sc_out[index] = value
        return [(at, send(sc_out.at[index], sc_in.at[at], peer)) for peer, at in zip(stage_peers, count)]

    def stage_end(value, copies):
        for at, copy in copies:
            copy.wait_recv()
            value = value + sc_in[at]
        return value

    for copy in w_copies + v_copies:
        copy.wait_recv()
    w = w_ref[...]
    row_at = iota((rb, NX), 0)
    col_at = iota((rb, NX), 1)
    zero = jnp.zeros((rb, NX), f32)
    w_up = jnp.where((row_at == 0) & (r == 0), zero, wext[7 : 7 + rb, :])
    w_down = jnp.where((row_at == rb - 1) & (r == nr - 1), zero, wext[9 : 9 + rb, :])
    w_left = jnp.where(col_at == 0, zero, pltpu.roll(w, 1, 1))
    w_right = jnp.where(col_at == NX - 1, zero, pltpu.roll(w, NX - 1, 1))
    w_prev = jnp.where(g == 0, zero, wgrp[0])
    w_next = jnp.where(g == ng - 1, zero, wgrp[1])
    power = jnp.zeros((1, 2 * SB), f32)
    energy = jnp.zeros((1, 2 * SB), f32)
    for ch in range(2):
        cols = slice(ch * NX, ch * NX + NX)
        v = vext[8 : 8 + rb, cols]
        total = w_up * (v - vext[7 : 7 + rb, cols])
        total += w_down * (v - vext[9 : 9 + rb, cols])
        total += w_left * (v - pltpu.roll(v, 1, 1))
        total += w_right * (v - pltpu.roll(v, NX - 1, 1))
        smoothed = reg_strength * (w * total) + damping * v
        lap_ref[:, cols] = smoothed
        power = power + jnp.sum(v * v, axis=0, keepdims=True)
        energy = energy + jnp.sum(v * smoothed, axis=0, keepdims=True)
        step = v[:hb] - vgrp[1, :hb, cols]
        edges = jnp.sum(w[:hb] * w_next[:hb] * (step * step), axis=0, keepdims=True)
        step = v[hb:] - vgrp[0, hb:, cols]
        edges += jnp.sum(w[hb:] * w_prev[hb:] * (step * step), axis=0, keepdims=True)
        energy = energy + reg_strength * edges
    power = power[:, :SB] + power[:, SB:]
    energy = energy[:, :SB] + energy[:, SB:]
    first_row = iota((2, SB), 0) == 0
    tile_sum = jnp.where(first_row, power, energy)
    across = stage_start(0, tile_sum, band_peer)

    tot = own_sum[...]
    for o in range(1, nb):
        bands[o - 1].wait_recv()
        tot = tot + band_in[o]
    own_tot[...] = tot
    back = send(own_tot, v_tot.at[pl.ds(64, 64)], partner)
    v_tot[0:64, :] = tot
    tile_sum = stage_end(tile_sum, across)
    tile_sum = tile_sum + jnp.where(first_row, 0.0, jnp.sum(tot * tot, axis=0, keepdims=True))
    plane = stage_start(1, tile_sum, plane_peer)

    factors = [spread(from_ref(v_tot), 0), spread(from_ref(v_tot), 1)]
    back.wait_recv()
    factors += [spread(from_ref(v_tot), 2), spread(from_ref(v_tot), 3)]
    tile_sum = stage_end(tile_sum, plane)
    along = stage_start(2, tile_sum, line_peer)
    part2[pl.ds(far, 128), :] = row_stage(factors, range(4), far)
    sent = scatter(part2, rs2, True)
    part2[pl.ds(near, 128), :] = row_stage(factors, range(4), near)
    sent.update(scatter(part2, rs2, False))
    for copy in late_copies:
        copy.wait_recv()
    for ch in range(2):
        cols = slice(ch * NX, ch * NX + NX)
        v = vext[8 : 8 + rb, cols]
        total = w_prev * (v - vgrp[0, :, cols]) + w_next * (v - vgrp[1, :, cols])
        lap_ref[:, cols] += reg_strength * (w * total)
    same, diff = collect(part2, rs2, sent)
    tile_sum = stage_end(tile_sum, along)
    totals = jnp.sum(tile_sum, axis=1, keepdims=True)
    alpha = totals[0:1] / totals[1:2]
    for at, piece in enumerate(widen(same, diff)):
        cols = slice(at * HALF, at * HALF + HALF)
        v = vext[8 : 8 + rb, cols]
        x_ref[:, cols] = alpha * v
        res_ref[:, cols] = v - alpha * (piece + lap_ref[:, cols])
    for copy in started:
        copy.wait_send()


def on_device(
    dims, kspace_data, coil_maps, smooth_weight, kernel_cols, kernel_rows, tile_index, caipi_cycle
):
    nb, ny, nz, nr = dims
    rb = NY // nr
    vmem = pl.BlockSpec(memory_space=pltpu.VMEM)
    smem = pl.BlockSpec(memory_space=pltpu.SMEM)
    anywhere = pl.BlockSpec(memory_space=pl.ANY)
    field = jax.ShapeDtypeStruct((rb, 2 * NX), f32)
    solution_field, residual = pl.pallas_call(
        functools.partial(kernel, dims),
        out_shape=(field, field),
        in_specs=[anywhere, anywhere, anywhere, anywhere, anywhere, smem, smem],
        out_specs=(vmem, vmem),
        scratch_shapes=[
            pltpu.VMEM((2, NY, 2 * NX), bf16),
            pltpu.VMEM((2, NY, NX), f32),
            pltpu.VMEM((4, NY, NX), f32),
            pltpu.VMEM((2, 2, NBLK * SB), f32),
            pltpu.VMEM((2, 2, NBLK * SB), f32),
            pltpu.VMEM((rb, NX), f32),
            pltpu.VMEM((16, NBLK * SB), bf16),
            pltpu.VMEM((16, NBLK * SB), bf16),
            pltpu.VMEM((2, 256, 768), bf16),
            pltpu.VMEM((512, 768), bf16),
            pltpu.VMEM((2, 384, 256), bf16),
            pltpu.VMEM((2, 768, 256), bf16),
            pltpu.VMEM((2, 128, 256), bf16),
            pltpu.VMEM((2, 256, SB), bf16),
            pltpu.VMEM((256, SB), f32),
            pltpu.VMEM((128, SB), f32),
            pltpu.VMEM((128, SB), f32),
            pltpu.VMEM((64, SB), f32),
            pltpu.VMEM((64, SB), f32),
            pltpu.VMEM((nb, 64, SB), f32),
            pltpu.VMEM((64, SB), f32),
            pltpu.VMEM((NY, NX), f32),
            pltpu.VMEM((NY, NX), f32),
            pltpu.VMEM((nr, rb, NX), f32),
            pltpu.VMEM((nr, rb, NX), f32),
            pltpu.VMEM((2, rb, NX), f32),
            pltpu.VMEM((NY, NX), f32),
            pltpu.VMEM((rb + 16, 2 * NX), f32),
            pltpu.VMEM((2, rb, 2 * NX), f32),
            pltpu.VMEM((rb + 16, NX), f32),
            pltpu.VMEM((2, rb, NX), f32),
            pltpu.VMEM((rb, 2 * NX), f32),
            pltpu.VMEM((3, 2, SB), f32),
            pltpu.VMEM((32, 2, SB), f32),
            pltpu.SemaphoreType.DMA((80,)),
            pltpu.SemaphoreType.DMA((80,)),
            pltpu.SemaphoreType.DMA((5,)),
        ],
        compiler_params=pltpu.CompilerParams(
            collective_id=0, has_side_effects=True, vmem_limit_bytes=67043328
        ),
    )(
        coil_maps[0, 0],
        kspace_data[0],
        smooth_weight[0, 0],
        kernel_cols.T,
        kernel_rows.T,
        tile_index,
        caipi_cycle,
    )
    return solution_field[None, None], residual[None, None]


def solution(mesh, split_grp=(4, 4)):
    dims = (mesh.shape["band"],) + tuple(split_grp) + (mesh.shape["row"],)
    return jax.shard_map(
        functools.partial(on_device, dims),
        mesh=mesh,
        in_specs=(
            P("grp", "row", None, None),
            P("band", "grp", "row", None, None),
            P("band", "grp", "row", None),
            P(),
            P(),
            P(),
            P("band"),
        ),
        out_specs=(P("band", "grp", "row", None), P("band", "grp", "row", None)),
        check_vma=False,
    )
```

```python
import functools
import math

import jax
import jax.numpy as jnp
from jax import lax
from jax.experimental import pallas as pl
from jax.experimental.pallas import tpu as pltpu
from jax.sharding import PartitionSpec as P

NY = 256
NX = 256
TY = 16
TX = 16
SB = 128
NBLK = 16
HALF = NX // 2

reg_strength = 0.5
damping = 1.0
f32 = jnp.float32
bf16 = jnp.bfloat16
MESH = pl.DeviceIdType.MESH


def cos_turn(n):
    n = n - 256.0 * jnp.floor(n * (1.0 / 256.0))
    t = (jnp.abs(n - 128.0) - 64.0) * (2.0 * math.pi / 256.0)
    u = t * t
    series = -1.0 / math.factorial(11)
    for order, sign in ((9, 1.0), (7, -1.0), (5, 1.0), (3, -1.0), (1, 1.0)):
        series = sign / math.factorial(order) + u * series
    return t * series


def sin_turn(n):
    return cos_turn(n + 192.0)


def split(x):
    high = x.astype(bf16)
    return high, (x - high.astype(f32)).astype(bf16)


def mm(a, b):
    return jnp.dot(a, b, preferred_element_type=f32)


def mm_nt(a, b):
    return lax.dot_general(a, b, (((1,), (1,)), ((), ())), preferred_element_type=f32)


def iota(shape, axis):
    return lax.broadcasted_iota(jnp.int32, shape, axis)


def kernel(
    dims,
    coil_hbm,
    ks_hbm,
    w_hbm,
    kc_hbm,
    kr_hbm,
    tile_hbm,
    caipi_ref,
    out_ref,
    tile_ref,
    coil_v,
    coil_send,
    coil_buf,
    ks_own,
    ks_part,
    w_ref,
    kc_v,
    kr_v,
    row_p,
    row_k,
    col_q,
    col_f,
    kc_nt,
    kc_nn,
    kr2,
    v_in,
    v_ref,
    v_tot,
    pair_in,
    own_sum,
    band_in,
    own_tot,
    part1,
    part2,
    rs1,
    rs2,
    gsum,
    rg,
    vext,
    vgrp,
    wext,
    wgrp,
    lap_ref,
    sc_out,
    sc_in,
    ssem,
    rsem,
    lsem,
    hello,
):
    nb, ny, nz, nr = dims
    ng = ny * nz
    nl = nr // 2
    rb = NY // nr
    b = lax.axis_index("band")
    g = lax.axis_index("grp")
    r = lax.axis_index("row")
    h = lax.rem(r, 2)
    zl = lax.div(r, 2)
    gy = lax.div(g, nz)
    gz = lax.rem(g, nz)
    partner = {"row": r + 1 - 2 * h}
    band_peer = [{"band": lax.rem(b + o, nb)} for o in range(1, nb)]
    plane_peer = [
        {
            "band": lax.rem(b + i, nb),
            "grp": lax.rem(gy + j, ny) * nz + gz,
            "row": zl * 2 + lax.rem(h + k, 2),
        }
        for i in range(nb)
        for j in range(ny)
        for k in range(2)
        if i or j or k
    ]
    line = gz * nl + zl
    line_peer = []
    for o in range(1, nz * nl):
        at = lax.rem(line + o, nz * nl)
        line_peer.append({"grp": gy * nz + lax.div(at, nl), "row": lax.rem(at, nl) * 2 + h})
    g_next = {"grp": lax.rem(g + 1, ng)}
    g_prev = {"grp": lax.rem(g + ng - 1, ng)}
    across = [{"row": lax.rem(zl + o, nl) * 2 + 1 - h} for o in range(1, nl)]
    across = [{"row": lax.rem(zl + o, nl) * 2 + 1 - h} for o in range(1, nl)]
    size = nz * nl
    reach = size // 4
    near_line = [line_peer[o - 1] for o in range(1, size) if min(o, size - o) <= reach]
    hello_peer = [line_peer[reach - 1], line_peer[size - reach - 1]]
    peers = near_line + [g_next, g_prev] + plane_peer + across

    barrier = pltpu.get_barrier_semaphore()
    for peer in peers:
        pl.semaphore_signal(barrier, inc=1, device_id=peer, device_id_type=MESH)
    fetches = [
        pltpu.make_async_copy(src, dst, lsem.at[at])
        for at, (src, dst) in enumerate(
            (
                (tile_hbm, tile_ref),
                (kc_hbm, kc_v),
                (kr_hbm, kr_v),
                (ks_hbm, ks_own),
                (coil_hbm, coil_v),
                (w_hbm, w_ref),
            )
        )
    ]
    for copy in fetches:
        copy.start()

    slots = iter(range(64))

    def exchange(copies, sized):
        slot = next(slots)
        for src, dst, peer in copies:
            pltpu.make_async_remote_copy(
                src_ref=src,
                dst_ref=dst,
                send_sem=ssem.at[slot],
                recv_sem=rsem.at[slot],
                device_id=peer,
                device_id_type=MESH,
            ).start()
        whole = pltpu.make_async_remote_copy(
            src_ref=sized,
            dst_ref=sized,
            send_sem=ssem.at[slot],
            recv_sem=rsem.at[slot],
            device_id=partner,
            device_id_type=MESH,
        )
        started.append(whole)
        return whole

    started = []

    def send(src, dst, peer):
        return exchange([(src, dst, peer)], dst)

    hb = rb // 2

    def row_at_place(place):
        inside = jnp.bitwise_and(place, 127)
        return (
            lax.shift_right_logical(inside, hb.bit_length() - 1) * rb
            + lax.shift_right_logical(place, 7) * hb
            + jnp.bitwise_and(inside, hb - 1)
        )

    lane = iota((1, 256), 1)
    lane_f = lax.shift_right_logical(jnp.bitwise_and(lane, 127), 3).astype(f32)
    lane_m = jnp.zeros((1, 256), f32)
    lane_c = jnp.bitwise_and(lane, 15).astype(f32)
    row_block = jnp.bitwise_and(lane, 7) + 8 * lax.shift_right_logical(lane, 7)
    col_block = lax.shift_right_logical(lane, 4)
    q_half = (iota((16, HALF), 1) + h * HALF).astype(f32)
    p_lane = row_at_place(iota((16, 256), 1)).astype(f32)
    sub16_q = iota((16, HALF), 0).astype(f32)
    sub = iota((16, 256), 0)
    sub_block = jnp.bitwise_and(sub, 7)
    sub_row = lax.shift_right_logical(sub, 3).astype(f32)
    scale = 1.0 / 16.0
    fetches[0].wait()
    cycle = caipi_ref[0]
    for half in range(2):
        sub_f = sub_row
        sub_m = jnp.zeros((16, 256), f32)
        for k in range(half * 8, half * 8 + 8):
            tile = tile_ref[k]
            ty = jnp.right_shift(tile, 4).astype(f32) * 16.0
            tx = jnp.bitwise_and(tile, 15).astype(f32) * 16.0
            turns = 256.0 - 64.0 * jnp.bitwise_and(cycle * k, 3).astype(f32)
            lane_f = jnp.where(row_block == k, lane_f + ty, lane_f)
            lane_m = jnp.where(row_block == k, turns, lane_m)
            lane_c = jnp.where(col_block == k, lane_c + tx, lane_c)
            sub_f = jnp.where(sub_block == k % 8, sub_f + ty, sub_f)
            sub_m = jnp.where(sub_block == k % 8, turns, sub_m)
            turn = q_half * (sub16_q + tx)
            at = (k % 8) * 16
            for part, values in ((0, cos_turn(turn)), (1, sin_turn(turn))):
                high, low = split(values * scale)
                to = slice(part * HALF, part * HALF + HALF)
                col_q[half, at : at + 16, to] = high
                col_q[half, 128 + at : 128 + at + 16, to] = low
                col_q[half, 256 + at : 256 + at + 16, to] = high
        for y in range(0, 16, 2):
            turn = p_lane * (sub_f + float(y)) + sub_m
            for part, values in ((0, cos_turn(turn)), (1, sin_turn(turn))):
                high, low = split(values * scale)
                at = part * 256 + half * 128 + y * 8
                row_k[at : at + 16, 0:256] = high
                row_k[at : at + 16, 256:512] = high
                row_k[at : at + 16, 512:768] = low
    turn = row_at_place(iota((256, 256), 0)).astype(f32) * lane_f + lane_m
    for part, values in ((0, cos_turn(turn)), (1, sin_turn(turn))):
        high, low = split(values * scale)
        row_p[part, :, 0:256] = high
        row_p[part, :, 256:512] = high
        row_p[part, :, 512:768] = low
    turn = (iota((HALF, 256), 0) + h * HALF).astype(f32) * lane_c
    cosine, sine = cos_turn(turn) * scale, sin_turn(turn) * scale
    levels = tuple(zip(split(cosine), split(sine)))
    for third, level in enumerate((0, 1, 0)):
        cos_part, sin_part = levels[level]
        at = third * 256
        for half in range(2):
            cols = slice(half * 128, half * 128 + 128)
            col_f[half, at : at + 128, 0:128] = cos_part[:, cols]
            col_f[half, at : at + 128, 128:256] = -sin_part[:, cols]
            col_f[half, at + 128 : at + 256, 0:128] = sin_part[:, cols]
            col_f[half, at + 128 : at + 256, 128:256] = cos_part[:, cols]
    fetches[1].wait()
    fetches[2].wait()
    for k in range(NBLK):
        half, at = k // 8, (k % 8) * 16
        cols = slice(k * SB, k * SB + SB)
        piece = kc_v[:, cols]
        kc_nt[half, at : at + 16, 0:SB] = piece
        kc_nt[half, at : at + 16, SB : 2 * SB] = piece
        kc_nn[half, at : at + 16, :] = piece
        kc_nn[half, 128 + at : 128 + at + 16, :] = piece
        kr2[pl.ds(half * 128 + k % 8, 16, stride=8), :] = kr_v[:, cols].astype(f32)
    keep = (
        jnp.bitwise_and(iota((128, 128), 0), 7)
        == lax.shift_right_logical(iota((128, 128), 1), 4)
    )
    keep4 = jnp.concatenate([keep] * 4, axis=0)

    def spread(ref, first):
        blocks = [[], []]
        for half in range(2):
            weights = kr2[half * 128 : half * 128 + 128, :].reshape(16, 8, SB)
            pieces = []
            for at in range(4):
                at = (first * 2 + at) * NBLK + half * 8
                pieces.append((weights * ref[at : at + 8, :][None]).reshape(128, SB))
            high, low = split(jnp.concatenate(pieces, axis=0))
            tiles = mm_nt(jnp.concatenate([high, low], axis=1), kc_nt[half])
            high, low = split(jnp.where(keep4, tiles, 0.0))
            mixed = mm(jnp.concatenate([high, high, low], axis=1), col_q[half])
            for c in range(2):
                real, imag = mixed[c * 256 : c * 256 + 128], mixed[c * 256 + 128 : c * 256 + 256]
                blocks[c].append(
                    jnp.concatenate(
                        [real[:, :HALF] - imag[:, HALF:], real[:, HALF:] + imag[:, :HALF]], axis=1
                    )
                )
        factors = []
        for c in range(2):
            high, low = split(jnp.concatenate(blocks[c], axis=0))
            factors.append(jnp.concatenate([high, low, high], axis=0))
        return factors

    def row_stage(factors, sub):
        rows = slice(sub * 128, sub * 128 + 128)
        left = jnp.concatenate([row_p[0, rows, :], row_p[1, rows, :]], axis=0)
        sum_r = sum_i = None
        for c, factor in enumerate(factors):
            mixed = mm(left, factor)
            im_r = mixed[:128, :HALF] - mixed[128:, HALF:]
            im_i = mixed[:128, HALF:] + mixed[128:, :HALF]
            coil_r, coil_i = coil_buf[c, rows, :HALF], coil_buf[c, rows, HALF:]
            term_r = coil_r * im_r + coil_i * im_i
            term_i = coil_r * im_i - coil_i * im_r
            sum_r = term_r if sum_r is None else sum_r + term_r
            sum_i = term_i if sum_i is None else sum_i + term_i
        return jnp.concatenate([sum_r, sum_i], axis=1)

    def by_block(samples, base):
        for c in range(2):
            for ch in range(2):
                for k in range(NBLK):
                    at = ((base + c) * 2 + ch) * NBLK + k
                    v_in[at : at + 1, :] = samples[c, ch : ch + 1, k * SB : k * SB + SB]

    targets = [lax.rem(r + o, nr) for o in range(1, nr)]

    def place_of(block, sub):
        return pl.ds(pl.multiple_of(sub * 128 + block * hb, hb), hb)

    def scatter(part, slots_in, sub):
        return exchange(
            [
                (part.at[place_of(to, sub)], slots_in.at[sub, o], {"row": to})
                for o, to in enumerate(targets)
            ],
            slots_in.at[sub, pl.ds(0, nr - 1)],
        )

    def collect(part, slots_in, sub):
        same, diff = part[place_of(r, sub), :], slots_in[sub, 0]
        for o in range(1, nr - 1):
            if o % 2:
                same = same + slots_in[sub, o]
            else:
                diff = diff + slots_in[sub, o]
        return same, diff

    def widen(same, diff):
        even = h == 0
        return (
            jnp.where(even, same[:, :HALF], diff[:, :HALF]),
            jnp.where(even, diff[:, :HALF], same[:, :HALF]),
            jnp.where(even, same[:, HALF:], diff[:, HALF:]),
            jnp.where(even, diff[:, HALF:], same[:, HALF:]),
        )


    fetches[3].wait()
    by_block(ks_own, 0)
    fetches[4].wait()

    def half_of(part, half):
        return pl.ds(pl.multiple_of(part * NX + half * HALF, HALF), HALF)

    for c in range(2):
        for part in range(2):
            to = slice(part * HALF, part * HALF + HALF)
            for place in range(0, NY, hb):
                block, sub = (place % 128) // hb, place // 128
                rows, at = slice(place, place + hb), slice(block * rb + sub * hb, block * rb + sub * hb + hb)
                coil_send[c, rows, to] = coil_v[c, at, half_of(part, 1 - h)].astype(f32)
                coil_buf[c, rows, to] = coil_v[c, at, half_of(part, h)].astype(f32)
    fetches[5].wait()
    wext[8 : 8 + rb, :] = w_ref[...]

    pl.semaphore_wait(barrier, len(peers))

    ks_copy = send(ks_own, ks_part, partner)
    partner_coils = send(coil_send, coil_buf.at[pl.ds(2, 2)], partner)
    w_copies = [
        send(w_ref, wgrp.at[0], g_next),
        send(w_ref, wgrp.at[1], g_prev),
        send(w_ref.at[pl.ds(rb - 8, 8)], wext.at[pl.ds(0, 8)], {"row": lax.rem(r + 1, nr)}),
        send(w_ref.at[pl.ds(0, 8)], wext.at[pl.ds(rb + 8, 8)], {"row": lax.rem(r + nr - 1, nr)}),
    ]
    for peer in hello_peer:
        pl.semaphore_signal(hello, inc=1, device_id=peer, device_id_type=MESH)
    factors = spread(v_in, 0)
    ks_copy.wait_recv()
    by_block(ks_part, 2)
    factors += spread(v_in, 2)
    partner_coils.wait_recv()
    part1[0:128, :] = row_stage(factors, 0)
    scattered = [scatter(part1, rs1, 0)]
    part1[128:256, :] = row_stage(factors, 1)
    scattered.append(scatter(part1, rs1, 1))
    gathered = []
    for sub in range(2):
        scattered[sub].wait_recv()
        same, diff = collect(part1, rs1, sub)
        gsum[sub, 0] = same
        gsum[sub, 1] = diff
        gathered.append(
            exchange(
                [
                    (gsum.at[sub, (o + 1) % 2], rg.at[place_of(r, sub)], {"row": to})
                    for o, to in enumerate(targets)
                ],
                rg.at[pl.ds(0, (nr - 1) * hb)],
            )
        )
        rg[place_of(r, sub), :] = same
        for at, piece in enumerate(widen(same, diff)):
            vext[8 + sub * hb : 8 + sub * hb + hb, at * HALF : at * HALF + HALF] = piece
    v_copies = [
        send(vext.at[pl.ds(rb, 8)], vext.at[pl.ds(0, 8)], {"row": lax.rem(r + 1, nr)}),
        send(vext.at[pl.ds(8, 8)], vext.at[pl.ds(rb + 8, 8)], {"row": lax.rem(r + nr - 1, nr)}),
    ]
    for copy in gathered:
        copy.wait_recv()
    v_copies += [
        send(vext.at[pl.ds(8, hb)], vgrp.at[1, pl.ds(0, hb)], g_prev),
        send(vext.at[pl.ds(8 + hb, hb)], vgrp.at[0, pl.ds(hb, hb)], g_next),
    ]
    late_copies = [
        send(vext.at[pl.ds(8 + hb, hb)], vgrp.at[1, pl.ds(hb, hb)], g_prev),
        send(vext.at[pl.ds(8, hb)], vgrp.at[0, pl.ds(0, hb)], g_next),
    ]

    image_r, image_i = rg[:, :HALF], rg[:, HALF:]
    pairs, bands = [], []

    def to_bands(batch):
        rows = slice(batch * 32, batch * 32 + 32)
        pairs[batch].wait_recv()
        own_sum[batch] = v_ref[rows, :] + pair_in[rows, :]
        bands.append(
            exchange(
                [(own_sum.at[batch], band_in.at[batch, o], peer) for o, peer in enumerate(band_peer)],
                band_in.at[batch, pl.ds(0, nb - 1)],
            )
        )

    for batch in range(2):
        lefts = []
        for c in (batch, batch + 2):
            coil_r, coil_i = coil_buf[c, :, :HALF], coil_buf[c, :, HALF:]
            high, low = split(
                jnp.concatenate(
                    [coil_r * image_r - coil_i * image_i, coil_r * image_i + coil_i * image_r],
                    axis=1,
                )
            )
            mixed = mm(row_k[...], jnp.concatenate([high, low, high], axis=0))
            high, low = split(
                jnp.concatenate(
                    [
                        mixed[:256, :HALF] + mixed[256:, HALF:],
                        mixed[:256, HALF:] - mixed[256:, :HALF],
                    ],
                    axis=1,
                )
            )
            lefts.append(jnp.concatenate([high, high, low], axis=1))
        for half in range(2):
            rows = slice(half * 128, half * 128 + 128)
            grid = mm(jnp.concatenate([left[rows] for left in lefts], axis=0), col_f[half])
            parts = [grid[c * 128 : c * 128 + 128, ch * 128 : ch * 128 + 128] for c in range(2) for ch in range(2)]
            high, low = split(jnp.where(keep4, jnp.concatenate(parts, axis=0), 0.0))
            sampled = mm(jnp.concatenate([high, low], axis=1), kc_nn[half])
            for at in range(4):
                weighted = sampled[at * 128 : at * 128 + 128] * kr2[rows, :]
                to = (batch + at // 2 * 2) * 32 + at % 2 * NBLK + half * 8
                v_ref[to : to + 8, :] = jnp.sum(weighted.reshape(16, 8, SB), axis=0)
            if batch == 1 and half == 0:
                to_bands(0)
        pairs.append(
            send(v_ref.at[pl.ds(64 + batch * 32, 32)], pair_in.at[pl.ds(batch * 32, 32)], partner)
        )
    to_bands(1)

    def stage_start(index, base, value, stage_peers):
        sc_out[index] = value
        return exchange(
            [(sc_out.at[index], sc_in.at[base + o], peer) for o, peer in enumerate(stage_peers)],
            sc_in.at[pl.ds(base, len(stage_peers))],
        )

    def stage_end(base, value, copies, count):
        copies.wait_recv()
        return value + jnp.sum(sc_in[base : base + count], axis=0)

    tots = []
    for batch in range(2):
        bands[batch].wait_recv()
        part = own_sum[batch]
        for o in range(nb - 1):
            part = part + band_in[batch, o]
        tots.append(part)
    tot = jnp.concatenate(tots, axis=0)
    own_tot[...] = tot
    back = send(own_tot, v_tot.at[pl.ds(64, 64)], partner)
    v_tot[0:64, :] = tot
    squares = jnp.sum(tot * tot, axis=0, keepdims=True) * (1.0 / nb)

    factors = spread(v_tot, 0)
    for copy in w_copies + v_copies:
        copy.wait_recv()
    w = w_ref[...]
    row_at = iota((rb, NX), 0)
    col_at = iota((rb, NX), 1)
    zero = jnp.zeros((rb, NX), f32)
    w_up = jnp.where((row_at == 0) & (r == 0), zero, wext[7 : 7 + rb, :])
    w_down = jnp.where((row_at == rb - 1) & (r == nr - 1), zero, wext[9 : 9 + rb, :])
    w_left = jnp.where(col_at == 0, zero, pltpu.roll(w, 1, 1))
    w_right = jnp.where(col_at == NX - 1, zero, pltpu.roll(w, NX - 1, 1))
    w_prev = jnp.where(g == 0, zero, wgrp[0])
    w_next = jnp.where(g == ng - 1, zero, wgrp[1])
    power = jnp.zeros((1, 2 * SB), f32)
    energy = jnp.zeros((1, 2 * SB), f32)
    for ch in range(2):
        cols = slice(ch * NX, ch * NX + NX)
        v = vext[8 : 8 + rb, cols]
        total = w_up * (v - vext[7 : 7 + rb, cols])
        total += w_down * (v - vext[9 : 9 + rb, cols])
        total += w_left * (v - pltpu.roll(v, 1, 1))
        total += w_right * (v - pltpu.roll(v, NX - 1, 1))
        smoothed = reg_strength * (w * total) + damping * v
        lap_ref[:, cols] = smoothed
        power = power + jnp.sum(v * v, axis=0, keepdims=True)
        energy = energy + jnp.sum(v * smoothed, axis=0, keepdims=True)
        step = v[:hb] - vgrp[1, :hb, cols]
        edges = jnp.sum(w[:hb] * w_next[:hb] * (step * step), axis=0, keepdims=True)
        step = v[hb:] - vgrp[0, hb:, cols]
        edges += jnp.sum(w[hb:] * w_prev[hb:] * (step * step), axis=0, keepdims=True)
        energy = energy + reg_strength * edges
    power = power[:, :SB] + power[:, SB:]
    energy = energy[:, :SB] + energy[:, SB:]
    first_row = iota((2, SB), 0) == 0
    tile_sum = jnp.where(first_row, power, energy)
    tile_sum = tile_sum + jnp.where(first_row, 0.0, squares)
    plane = stage_start(0, 0, tile_sum, plane_peer)
    back.wait_recv()
    factors += spread(v_tot, 2)
    part2[0:128, :] = row_stage(factors, 0)
    scattered = [scatter(part2, rs2, 0)]
    part2[128:256, :] = row_stage(factors, 1)
    tile_sum = stage_end(0, tile_sum, plane, len(plane_peer))
    pl.semaphore_wait(hello, len(hello_peer))
    along = stage_start(1, len(plane_peer), tile_sum, line_peer)
    scattered.append(scatter(part2, rs2, 1))
    for copy in late_copies:
        copy.wait_recv()
    for ch in range(2):
        cols = slice(ch * NX, ch * NX + NX)
        v = vext[8 : 8 + rb, cols]
        total = w_prev * (v - vgrp[0, :, cols]) + w_next * (v - vgrp[1, :, cols])
        lap_ref[:, cols] += reg_strength * (w * total)
    for copy in scattered:
        copy.wait_recv()
    tile_sum = stage_end(len(plane_peer), tile_sum, along, len(line_peer))
    totals = jnp.sum(tile_sum, axis=1, keepdims=True)
    alpha = totals[0:1] / totals[1:2]
    for sub in range(2):
        rows = slice(sub * hb, sub * hb + hb)
        for at, piece in enumerate(widen(*collect(part2, rs2, sub))):
            cols = slice(at * HALF, at * HALF + HALF)
            v = vext[8 + sub * hb : 8 + sub * hb + hb, cols]
            out_ref[0, rows, cols] = alpha * v
            out_ref[1, rows, cols] = v - alpha * (piece + lap_ref[rows, cols])
    for copy in started:
        copy.wait_send()


def on_device(
    dims, kspace_data, coil_maps, smooth_weight, kernel_cols, kernel_rows, tile_index, caipi_cycle
):
    nb, ny, nz, nr = dims
    rb = NY // nr
    vmem = pl.BlockSpec(memory_space=pltpu.VMEM)
    hbm = pl.BlockSpec(memory_space=pltpu.HBM)
    fields = pl.pallas_call(
        functools.partial(kernel, dims),
        out_shape=jax.ShapeDtypeStruct((2, rb, 2 * NX), f32),
        in_specs=[hbm] * 6 + [pl.BlockSpec(memory_space=pltpu.SMEM)],
        out_specs=vmem,
        scratch_shapes=[
            pltpu.SMEM((NBLK,), jnp.int32),
            pltpu.VMEM((2, NY, 2 * NX), bf16),
            pltpu.VMEM((2, NY, NX), f32),
            pltpu.VMEM((4, NY, NX), f32),
            pltpu.VMEM((2, 2, NBLK * SB), f32),
            pltpu.VMEM((2, 2, NBLK * SB), f32),
            pltpu.VMEM((rb, NX), f32),
            pltpu.VMEM((16, NBLK * SB), bf16),
            pltpu.VMEM((16, NBLK * SB), bf16),
            pltpu.VMEM((2, 256, 768), bf16),
            pltpu.VMEM((512, 768), bf16),
            pltpu.VMEM((2, 384, 256), bf16),
            pltpu.VMEM((2, 768, 256), bf16),
            pltpu.VMEM((2, 128, 256), bf16),
            pltpu.VMEM((2, 256, SB), bf16),
            pltpu.VMEM((256, SB), f32),
            pltpu.VMEM((128, SB), f32),
            pltpu.VMEM((128, SB), f32),
            pltpu.VMEM((128, SB), f32),
            pltpu.VMEM((64, SB), f32),
            pltpu.VMEM((2, 32, SB), f32),
            pltpu.VMEM((2, nb - 1, 32, SB), f32),
            pltpu.VMEM((64, SB), f32),
            pltpu.VMEM((NY, NX), f32),
            pltpu.VMEM((NY, NX), f32),
            pltpu.VMEM((2, nr - 1, rb // 2, NX), f32),
            pltpu.VMEM((2, nr - 1, rb // 2, NX), f32),
            pltpu.VMEM((2, 2, rb // 2, NX), f32),
            pltpu.VMEM((NY, NX), f32),
            pltpu.VMEM((rb + 16, 2 * NX), f32),
            pltpu.VMEM((2, rb, 2 * NX), f32),
            pltpu.VMEM((rb + 16, NX), f32),
            pltpu.VMEM((2, rb, NX), f32),
            pltpu.VMEM((rb, 2 * NX), f32),
            pltpu.VMEM((2, 2, SB), f32),
            pltpu.VMEM((64, 2, SB), f32),
            pltpu.SemaphoreType.DMA((25,)),
            pltpu.SemaphoreType.DMA((25,)),
            pltpu.SemaphoreType.DMA((6,)),
            pltpu.SemaphoreType.REGULAR,
        ],
        compiler_params=pltpu.CompilerParams(
            collective_id=0, has_side_effects=True, vmem_limit_bytes=48 * 1024 * 1024
        ),
    )(
        *(
            pltpu.with_memory_space_constraint(operand, pltpu.HBM)
            for operand in (
                coil_maps[0, 0],
                kspace_data[0],
                smooth_weight[0, 0],
                kernel_cols.T,
                kernel_rows.T,
                tile_index,
            )
        ),
        caipi_cycle,
    )
    return fields[0][None, None], fields[1][None, None]


def solution(mesh, split_grp=(4, 4)):
    dims = (mesh.shape["band"],) + tuple(split_grp) + (mesh.shape["row"],)
    return jax.shard_map(
        functools.partial(on_device, dims),
        mesh=mesh,
        in_specs=(
            P("grp", "row", None, None),
            P("band", "grp", "row", None, None),
            P("band", "grp", "row", None),
            P(),
            P(),
            P(),
            P("band"),
        ),
        out_specs=(P("band", "grp", "row", None), P("band", "grp", "row", None)),
        check_vma=False,
    )
```

```python
import functools
import math

import jax
import jax.numpy as jnp
from jax import lax
from jax.experimental import pallas as pl
from jax.experimental.pallas import tpu as pltpu
from jax.sharding import PartitionSpec as P

NY = 256
NX = 256
TY = 16
TX = 16
SB = 128
NBLK = 16
HALF = NX // 2

reg_strength = 0.5
damping = 1.0
f32 = jnp.float32
bf16 = jnp.bfloat16
MESH = pl.DeviceIdType.MESH


def cos_turn(n):
    n = n - 256.0 * jnp.floor(n * (1.0 / 256.0))
    t = (jnp.abs(n - 128.0) - 64.0) * (2.0 * math.pi / 256.0)
    u = t * t
    series = -1.0 / math.factorial(11)
    for order, sign in ((9, 1.0), (7, -1.0), (5, 1.0), (3, -1.0), (1, 1.0)):
        series = sign / math.factorial(order) + u * series
    return t * series


def sin_turn(n):
    return cos_turn(n + 192.0)


def split(x):
    high = x.astype(bf16)
    return high, (x - high.astype(f32)).astype(bf16)


def mm(a, b):
    return jnp.dot(a, b, preferred_element_type=f32)


def mm_nt(a, b):
    return lax.dot_general(a, b, (((1,), (1,)), ((), ())), preferred_element_type=f32)


def iota(shape, axis):
    return lax.broadcasted_iota(jnp.int32, shape, axis)


def kernel(
    dims,
    coil_hbm,
    ks_hbm,
    w_hbm,
    kc_hbm,
    kr_hbm,
    tile_hbm,
    caipi_ref,
    out_ref,
    tile_ref,
    coil_v,
    coil_send,
    coil_buf,
    ks_own,
    ks_part,
    w_ref,
    kc_v,
    kr_v,
    row_p,
    row_k,
    mixed_ref,
    col_q,
    col_f,
    kc_nt,
    kc_nn,
    kr2,
    v_in,
    v_ref,
    v_tot,
    pair_in,
    own_sum,
    band_in,
    own_tot,
    part1,
    part2,
    rs1,
    rs2,
    gsum,
    rg,
    vext,
    vgrp,
    wext,
    wgrp,
    lap_ref,
    sc_out,
    sc_in,
    ssem,
    rsem,
    lsem,
    hello,
):
    nb, ny, nz, nr = dims
    ng = ny * nz
    nl = nr // 2
    rb = NY // nr
    b = lax.axis_index("band")
    g = lax.axis_index("grp")
    r = lax.axis_index("row")
    h = lax.rem(r, 2)
    zl = lax.div(r, 2)
    gy = lax.div(g, nz)
    gz = lax.rem(g, nz)
    partner = {"row": r + 1 - 2 * h}
    band_peer = [{"band": lax.rem(b + o, nb)} for o in range(1, nb)]
    plane_peer = [
        {
            "band": lax.rem(b + i, nb),
            "grp": lax.rem(gy + j, ny) * nz + gz,
            "row": zl * 2 + lax.rem(h + k, 2),
        }
        for i in range(nb)
        for j in range(ny)
        for k in range(2)
        if i or j or k
    ]
    line = gz * nl + zl
    line_peer = []
    for o in range(1, nz * nl):
        at = lax.rem(line + o, nz * nl)
        line_peer.append({"grp": gy * nz + lax.div(at, nl), "row": lax.rem(at, nl) * 2 + h})
    g_next = {"grp": lax.rem(g + 1, ng)}
    g_prev = {"grp": lax.rem(g + ng - 1, ng)}
    across = [{"row": lax.rem(zl + o, nl) * 2 + 1 - h} for o in range(1, nl)]
    across = [{"row": lax.rem(zl + o, nl) * 2 + 1 - h} for o in range(1, nl)]
    size = nz * nl
    reach = size // 4
    near_line = [line_peer[o - 1] for o in range(1, size) if min(o, size - o) <= reach]
    hello_peer = [line_peer[reach - 1], line_peer[size - reach - 1]]
    peers = [g_next, g_prev] + near_line[reach - 1 : reach + 1] + plane_peer[::-1] + near_line[: reach - 1] + near_line[reach + 1 :] + across

    barrier = pltpu.get_barrier_semaphore()
    for peer in peers:
        pl.semaphore_signal(barrier, inc=1, device_id=peer, device_id_type=MESH)
    fetches = [
        pltpu.make_async_copy(src, dst, lsem.at[at])
        for at, (src, dst) in enumerate(
            (
                (tile_hbm, tile_ref),
                (kc_hbm, kc_v),
                (kr_hbm, kr_v),
                (ks_hbm, ks_own),
                (coil_hbm, coil_v),
                (w_hbm, w_ref),
            )
        )
    ]
    for copy in fetches:
        copy.start()

    slots = iter(range(64))

    def exchange(copies, sized):
        slot = next(slots)
        for src, dst, peer in copies:
            pltpu.make_async_remote_copy(
                src_ref=src,
                dst_ref=dst,
                send_sem=ssem.at[slot],
                recv_sem=rsem.at[slot],
                device_id=peer,
                device_id_type=MESH,
            ).start()
        whole = pltpu.make_async_remote_copy(
            src_ref=sized,
            dst_ref=sized,
            send_sem=ssem.at[slot],
            recv_sem=rsem.at[slot],
            device_id=partner,
            device_id_type=MESH,
        )
        started.append(whole)
        return whole

    started = []

    def send(src, dst, peer):
        return exchange([(src, dst, peer)], dst)

    hb = rb // 2

    def row_at_place(place):
        inside = jnp.bitwise_and(place, 127)
        return (
            lax.shift_right_logical(inside, hb.bit_length() - 1) * rb
            + lax.shift_right_logical(place, 7) * hb
            + jnp.bitwise_and(inside, hb - 1)
        )

    lane = iota((1, 256), 1)
    lane_f = lax.shift_right_logical(jnp.bitwise_and(lane, 127), 3).astype(f32)
    lane_m = jnp.zeros((1, 256), f32)
    lane_c = jnp.bitwise_and(lane, 15).astype(f32)
    row_block = jnp.bitwise_and(lane, 7) + 8 * lax.shift_right_logical(lane, 7)
    col_block = lax.shift_right_logical(lane, 4)
    q_half = (iota((16, HALF), 1) + h * HALF).astype(f32)
    p_lane = row_at_place(iota((16, 256), 1)).astype(f32)
    sub16_q = iota((16, HALF), 0).astype(f32)
    sub = iota((16, 256), 0)
    sub_block = jnp.bitwise_and(sub, 7)
    sub_row = lax.shift_right_logical(sub, 3).astype(f32)
    scale = 1.0 / 16.0
    fetches[0].wait()
    cycle = caipi_ref[0]
    for half in range(2):
        for k in range(half * 8, half * 8 + 8):
            tile = tile_ref[k]
            ty = jnp.right_shift(tile, 4).astype(f32) * 16.0
            tx = jnp.bitwise_and(tile, 15).astype(f32) * 16.0
            turns = 256.0 - 64.0 * jnp.bitwise_and(cycle * k, 3).astype(f32)
            lane_f = jnp.where(row_block == k, lane_f + ty, lane_f)
            lane_m = jnp.where(row_block == k, turns, lane_m)
            lane_c = jnp.where(col_block == k, lane_c + tx, lane_c)
            turn = q_half * (sub16_q + tx)
            at = (k % 8) * 16
            for part, values in ((0, cos_turn(turn)), (1, sin_turn(turn))):
                high, low = split(values * scale)
                to = slice(part * HALF, part * HALF + HALF)
                col_q[half, at : at + 16, to] = high
                col_q[half, 128 + at : 128 + at + 16, to] = low
                col_q[half, 256 + at : 256 + at + 16, to] = high
    turn = row_at_place(iota((256, 256), 0)).astype(f32) * lane_f + lane_m
    for part, values in ((0, cos_turn(turn)), (1, sin_turn(turn))):
        high, low = split(values * scale)
        row_p[part, :, 0:256] = high
        row_p[part, :, 256:512] = high
        row_p[part, :, 512:768] = low
    fetches[1].wait()
    fetches[2].wait()
    for k in range(NBLK):
        half, at = k // 8, (k % 8) * 16
        cols = slice(k * SB, k * SB + SB)
        piece = kc_v[:, cols]
        kc_nt[half, at : at + 16, 0:SB] = piece
        kc_nt[half, at : at + 16, SB : 2 * SB] = piece
        kc_nn[half, at : at + 16, :] = piece
        kc_nn[half, 128 + at : 128 + at + 16, :] = piece
        kr2[pl.ds(half * 128 + k % 8, 16, stride=8), :] = kr_v[:, cols].astype(f32)
    keep = (
        jnp.bitwise_and(iota((128, 128), 0), 7)
        == lax.shift_right_logical(iota((128, 128), 1), 4)
    )
    keep4 = jnp.concatenate([keep] * 4, axis=0)

    def spread(ref, first):
        halves = range(2)
        spreads = []
        for half in halves:
            weights = kr2[half * 128 : half * 128 + 128, :].reshape(16, 8, SB)
            pieces = []
            for at in range(4):
                at = (first * 2 + at) * NBLK + half * 8
                pieces.append((weights * ref[at : at + 8, :][None]).reshape(128, SB))
            spreads.append(jnp.concatenate(split(jnp.concatenate(pieces, axis=0)), axis=1))
        tiles = [mm_nt(spreads[half], kc_nt[half]) for half in halves]
        parts = [split(jnp.where(keep4, tiles[half], 0.0)) for half in halves]
        mixed = [
            mm(jnp.concatenate([high, high, low], axis=1), col_q[half])
            for half, (high, low) in zip(halves, parts)
        ]
        blocks = [[], []]
        for half in halves:
            for c in range(2):
                real = mixed[half][c * 256 : c * 256 + 128]
                imag = mixed[half][c * 256 + 128 : c * 256 + 256]
                blocks[c].append(
                    jnp.concatenate(
                        [real[:, :HALF] - imag[:, HALF:], real[:, HALF:] + imag[:, :HALF]], axis=1
                    )
                )
        factors = []
        for c in range(2):
            high, low = split(jnp.concatenate(blocks[c], axis=0))
            factors.append(jnp.concatenate([high, low, high], axis=0))
        return factors

    def row_stage(factors, sub, first=0, start=None):
        rows = slice(sub * 128, sub * 128 + 128)
        left = jnp.concatenate([row_p[0, rows, :], row_p[1, rows, :]], axis=0)
        sum_r, sum_i = (None, None) if start is None else (start[:, :HALF], start[:, HALF:])
        for c, factor in enumerate(factors, first):
            mixed = mm(left, factor)
            im_r = mixed[:128, :HALF] - mixed[128:, HALF:]
            im_i = mixed[:128, HALF:] + mixed[128:, :HALF]
            coil_r, coil_i = coil_buf[c, rows, :HALF], coil_buf[c, rows, HALF:]
            term_r = coil_r * im_r + coil_i * im_i
            term_i = coil_r * im_i - coil_i * im_r
            sum_r = term_r if sum_r is None else sum_r + term_r
            sum_i = term_i if sum_i is None else sum_i + term_i
        return jnp.concatenate([sum_r, sum_i], axis=1)

    def by_block(samples, base):
        for c in range(2):
            for ch in range(2):
                for k in range(NBLK):
                    at = ((base + c) * 2 + ch) * NBLK + k
                    v_in[at : at + 1, :] = samples[c, ch : ch + 1, k * SB : k * SB + SB]

    nq = nr // 2
    near_base = lax.div(r, nq) * nq
    order = [(nq - near_base, i) for i in range(nq)] + [(near_base, i) for i in range(1, nq)]
    targets = [base + lax.rem(lax.rem(r, nq) + i, nq) for base, i in order]
    crossed = [i % 2 for _, i in order]

    def place_of(block, sub):
        return pl.ds(pl.multiple_of(sub * 128 + block * hb, hb), hb)

    def scatter(part, slots_in, sub):
        return exchange(
            [
                (part.at[place_of(to, sub)], slots_in.at[sub, o], {"row": to})
                for o, to in enumerate(targets)
            ],
            slots_in.at[sub, pl.ds(0, nr - 1)],
        )

    def collect(part, slots_in, sub):
        sums = [part[place_of(r, sub), :], None]
        for o, other in enumerate(crossed):
            piece = slots_in[sub, o]
            sums[other] = piece if sums[other] is None else sums[other] + piece
        same, diff = sums
        return same, diff

    def widen(same, diff):
        even = h == 0
        return (
            jnp.where(even, same[:, :HALF], diff[:, :HALF]),
            jnp.where(even, diff[:, :HALF], same[:, :HALF]),
            jnp.where(even, same[:, HALF:], diff[:, HALF:]),
            jnp.where(even, diff[:, HALF:], same[:, HALF:]),
        )


    fetches[3].wait()
    by_block(ks_own, 0)
    fetches[4].wait()

    def half_of(part, half):
        return pl.ds(pl.multiple_of(part * NX + half * HALF, HALF), HALF)

    for c in range(2):
        for part in range(2):
            to = slice(part * HALF, part * HALF + HALF)
            for place in range(0, NY, hb):
                block, sub = (place % 128) // hb, place // 128
                rows, at = slice(place, place + hb), slice(block * rb + sub * hb, block * rb + sub * hb + hb)
                coil_send[c, rows, to] = coil_v[c, at, half_of(part, 1 - h)].astype(f32)
                coil_buf[c, rows, to] = coil_v[c, at, half_of(part, h)].astype(f32)
    factors = spread(v_in, 0)
    for sub in range(2):
        part1[sub * 128 : sub * 128 + 128, :] = row_stage(factors, sub)
    fetches[5].wait()
    wext[8 : 8 + rb, :] = w_ref[...]

    pl.semaphore_wait(barrier, len(peers))

    ks_copy = send(ks_own, ks_part, partner)
    partner_coils = send(coil_send, coil_buf.at[pl.ds(2, 2)], partner)
    w_copies = [
        send(w_ref.at[pl.ds(0, hb)], wgrp.at[1, pl.ds(0, hb)], g_prev),
        send(w_ref.at[pl.ds(hb, hb)], wgrp.at[0, pl.ds(hb, hb)], g_next),
        send(w_ref.at[pl.ds(rb - 8, 8)], wext.at[pl.ds(0, 8)], {"row": lax.rem(r + 1, nr)}),
        send(w_ref.at[pl.ds(0, 8)], wext.at[pl.ds(rb + 8, 8)], {"row": lax.rem(r + nr - 1, nr)}),
    ]
    for peer in hello_peer:
        pl.semaphore_signal(hello, inc=1, device_id=peer, device_id_type=MESH)
    ks_copy.wait_recv()
    by_block(ks_part, 2)
    factors = spread(v_in, 2)
    partner_coils.wait_recv()
    part1[0:128, :] = row_stage(factors, 0, 2, part1[0:128, :])
    scattered = [scatter(part1, rs1, 0)]
    part1[128:256, :] = row_stage(factors, 1, 2, part1[128:256, :])
    scattered.append(scatter(part1, rs1, 1))
    for half in range(2):
        sub_f = sub_row
        sub_m = jnp.zeros((16, 256), f32)
        for k in range(half * 8, half * 8 + 8):
            ty = jnp.right_shift(tile_ref[k], 4).astype(f32) * 16.0
            turns = 256.0 - 64.0 * jnp.bitwise_and(cycle * k, 3).astype(f32)
            sub_f = jnp.where(sub_block == k % 8, sub_f + ty, sub_f)
            sub_m = jnp.where(sub_block == k % 8, turns, sub_m)
        for y in range(0, 16, 2):
            turn = p_lane * (sub_f + float(y)) + sub_m
            for part, values in ((0, cos_turn(turn)), (1, sin_turn(turn))):
                high, low = split(values * scale)
                at = part * 256 + half * 128 + y * 8
                for sub_at in range(2):
                    cols = slice(sub_at * 128, sub_at * 128 + 128)
                    row_k[sub_at, at : at + 16, 0:128] = high[:, cols]
                    row_k[sub_at, at : at + 16, 128:256] = high[:, cols]
                    row_k[sub_at, at : at + 16, 256:384] = low[:, cols]
    turn = (iota((HALF, 256), 0) + h * HALF).astype(f32) * lane_c
    cosine, sine = cos_turn(turn) * scale, sin_turn(turn) * scale
    levels = tuple(zip(split(cosine), split(sine)))
    for third, level in enumerate((0, 1, 0)):
        cos_part, sin_part = levels[level]
        at = third * 256
        for half in range(2):
            cols = slice(half * 128, half * 128 + 128)
            col_f[half, at : at + 128, 0:128] = cos_part[:, cols]
            col_f[half, at : at + 128, 128:256] = -sin_part[:, cols]
            col_f[half, at + 128 : at + 256, 0:128] = sin_part[:, cols]
            col_f[half, at + 128 : at + 256, 128:256] = cos_part[:, cols]
    gathered = []
    for sub in range(2):
        scattered[sub].wait_recv()
        same, diff = collect(part1, rs1, sub)
        gsum[sub, 0] = same
        gsum[sub, 1] = diff
        gathered.append(
            exchange(
                [
                    (gsum.at[sub, crossed[o]], rg.at[place_of(r, sub)], {"row": to})
                    for o, to in enumerate(targets)
                ],
                rg.at[pl.ds(0, (nr - 1) * hb)],
            )
        )
        rg[place_of(r, sub), :] = same
        for at, piece in enumerate(widen(same, diff)):
            vext[8 + sub * hb : 8 + sub * hb + hb, at * HALF : at * HALF + HALF] = piece
    v_copies = [
        send(vext.at[pl.ds(rb, 8)], vext.at[pl.ds(0, 8)], {"row": lax.rem(r + 1, nr)}),
        send(vext.at[pl.ds(8, 8)], vext.at[pl.ds(rb + 8, 8)], {"row": lax.rem(r + nr - 1, nr)}),
    ]
    def frequencies(c, sub):
        rows = slice(sub * 128, sub * 128 + 128)
        coil_r, coil_i = coil_buf[c, rows, :HALF], coil_buf[c, rows, HALF:]
        image_r, image_i = rg[rows, :HALF], rg[rows, HALF:]
        high, low = split(
            jnp.concatenate(
                [coil_r * image_r - coil_i * image_i, coil_r * image_i + coil_i * image_r], axis=1
            )
        )
        return mm(row_k[sub], jnp.concatenate([high, low, high], axis=0))

    gathered[0].wait_recv()
    for c in range(4):
        mixed_ref[c] = frequencies(c, 0)
    gathered[1].wait_recv()
    v_copies += [
        send(vext.at[pl.ds(8, hb)], vgrp.at[1, pl.ds(0, hb)], g_prev),
        send(vext.at[pl.ds(8 + hb, hb)], vgrp.at[0, pl.ds(hb, hb)], g_next),
    ]

    for first in (2, 0):
        lefts = []
        for c in (first, first + 1):
            mixed = mixed_ref[c] + frequencies(c, 1)
            high, low = split(
                jnp.concatenate(
                    [
                        mixed[:256, :HALF] + mixed[256:, HALF:],
                        mixed[:256, HALF:] - mixed[256:, :HALF],
                    ],
                    axis=1,
                )
            )
            lefts.append(jnp.concatenate([high, high, low], axis=1))
        grids = [
            mm(
                jnp.concatenate([left[half * 128 : half * 128 + 128] for left in lefts], axis=0),
                col_f[half],
            )
            for half in range(2)
        ]
        sampled = []
        for half in range(2):
            parts = [
                grids[half][c * 128 : c * 128 + 128, ch * 128 : ch * 128 + 128]
                for c in range(2)
                for ch in range(2)
            ]
            high, low = split(jnp.where(keep4, jnp.concatenate(parts, axis=0), 0.0))
            sampled.append(mm(jnp.concatenate([high, low], axis=1), kc_nn[half]))
        for half in range(2):
            weights = kr2[half * 128 : half * 128 + 128, :]
            for at in range(4):
                weighted = sampled[half][at * 128 : at * 128 + 128] * weights
                to = (first * 2 + at) * NBLK + half * 8
                v_ref[to : to + 8, :] = jnp.sum(weighted.reshape(16, 8, SB), axis=0)
        if first == 2:
            pair = send(v_ref.at[pl.ds(64, 64)], pair_in, partner)
    pair.wait_recv()
    own_sum[...] = v_ref[0:64, :] + pair_in[...]
    bands = exchange(
        [(own_sum, band_in.at[o], peer) for o, peer in enumerate(band_peer)],
        band_in.at[pl.ds(0, nb - 1)],
    )

    late_copies = [
        send(w_ref.at[pl.ds(hb, hb)], wgrp.at[1, pl.ds(hb, hb)], g_prev),
        send(w_ref.at[pl.ds(0, hb)], wgrp.at[0, pl.ds(0, hb)], g_next),
        send(vext.at[pl.ds(8 + hb, hb)], vgrp.at[1, pl.ds(hb, hb)], g_prev),
        send(vext.at[pl.ds(8, hb)], vgrp.at[0, pl.ds(0, hb)], g_next),
    ]

    def stage_start(index, base, value, stage_peers):
        sc_out[index] = value
        return exchange(
            [(sc_out.at[index], sc_in.at[base + o], peer) for o, peer in enumerate(stage_peers)],
            sc_in.at[pl.ds(base, len(stage_peers))],
        )

    def stage_end(base, value, copies, count):
        copies.wait_recv()
        return value + jnp.sum(sc_in[base : base + count], axis=0)

    bands.wait_recv()
    tot = own_sum[...]
    for o in range(nb - 1):
        tot = tot + band_in[o]
    own_tot[...] = tot
    back = send(own_tot, v_tot.at[pl.ds(64, 64)], partner)
    v_tot[0:64, :] = tot
    squares = jnp.sum(tot * tot, axis=0, keepdims=True) * (1.0 / nb)

    for copy in w_copies + v_copies:
        copy.wait_recv()
    w = w_ref[...]
    row_at = iota((rb, NX), 0)
    col_at = iota((rb, NX), 1)
    zero = jnp.zeros((rb, NX), f32)
    w_up = jnp.where((row_at == 0) & (r == 0), zero, wext[7 : 7 + rb, :])
    w_down = jnp.where((row_at == rb - 1) & (r == nr - 1), zero, wext[9 : 9 + rb, :])
    w_left = jnp.where(col_at == 0, zero, pltpu.roll(w, 1, 1))
    w_right = jnp.where(col_at == NX - 1, zero, pltpu.roll(w, NX - 1, 1))
    part = zero[:hb]
    w_next_edge = jnp.where(g == ng - 1, part, wgrp[1, :hb])
    w_prev_edge = jnp.where(g == 0, part, wgrp[0, hb:])
    power = jnp.zeros((1, 2 * SB), f32)
    energy = jnp.zeros((1, 2 * SB), f32)
    for ch in range(2):
        cols = slice(ch * NX, ch * NX + NX)
        v = vext[8 : 8 + rb, cols]
        total = w_up * (v - vext[7 : 7 + rb, cols])
        total += w_down * (v - vext[9 : 9 + rb, cols])
        total += w_left * (v - pltpu.roll(v, 1, 1))
        total += w_right * (v - pltpu.roll(v, NX - 1, 1))
        smoothed = reg_strength * (w * total) + damping * v
        lap_ref[:, cols] = smoothed
        power = power + jnp.sum(v * v, axis=0, keepdims=True)
        energy = energy + jnp.sum(v * smoothed, axis=0, keepdims=True)
        step = v[:hb] - vgrp[1, :hb, cols]
        edges = jnp.sum(w[:hb] * w_next_edge * (step * step), axis=0, keepdims=True)
        step = v[hb:] - vgrp[0, hb:, cols]
        edges += jnp.sum(w[hb:] * w_prev_edge * (step * step), axis=0, keepdims=True)
        energy = energy + reg_strength * edges
    power = power[:, :SB] + power[:, SB:]
    energy = energy[:, :SB] + energy[:, SB:]
    first_row = iota((2, SB), 0) == 0
    tile_sum = jnp.where(first_row, power, energy)
    tile_sum = tile_sum + jnp.where(first_row, 0.0, squares)
    plane = stage_start(0, 0, tile_sum, plane_peer)
    factors = spread(v_tot, 0)
    back.wait_recv()
    factors += spread(v_tot, 2)
    part2[0:128, :] = row_stage(factors, 0)
    scattered = [scatter(part2, rs2, 0)]
    part2[128:256, :] = row_stage(factors, 1)
    scattered.append(scatter(part2, rs2, 1))
    tile_sum = stage_end(0, tile_sum, plane, len(plane_peer))
    pl.semaphore_wait(hello, len(hello_peer))
    along = stage_start(1, len(plane_peer), tile_sum, line_peer)
    for copy in late_copies:
        copy.wait_recv()
    w_prev = jnp.where(g == 0, zero, wgrp[0])
    w_next = jnp.where(g == ng - 1, zero, wgrp[1])
    for ch in range(2):
        cols = slice(ch * NX, ch * NX + NX)
        v = vext[8 : 8 + rb, cols]
        total = w_prev * (v - vgrp[0, :, cols]) + w_next * (v - vgrp[1, :, cols])
        lap_ref[:, cols] += reg_strength * (w * total)
    for copy in scattered:
        copy.wait_recv()
    tile_sum = stage_end(len(plane_peer), tile_sum, along, len(line_peer))
    totals = jnp.sum(tile_sum, axis=1, keepdims=True)
    alpha = totals[0:1] / totals[1:2]
    for sub in range(2):
        rows = slice(sub * hb, sub * hb + hb)
        for at, piece in enumerate(widen(*collect(part2, rs2, sub))):
            cols = slice(at * HALF, at * HALF + HALF)
            v = vext[8 + sub * hb : 8 + sub * hb + hb, cols]
            out_ref[0, rows, cols] = alpha * v
            out_ref[1, rows, cols] = v - alpha * (piece + lap_ref[rows, cols])
    for copy in started:
        copy.wait_send()


def on_device(
    dims, kspace_data, coil_maps, smooth_weight, kernel_cols, kernel_rows, tile_index, caipi_cycle
):
    nb, ny, nz, nr = dims
    rb = NY // nr
    vmem = pl.BlockSpec(memory_space=pltpu.VMEM)
    hbm = pl.BlockSpec(memory_space=pltpu.HBM)
    fields = pl.pallas_call(
        functools.partial(kernel, dims),
        out_shape=jax.ShapeDtypeStruct((2, rb, 2 * NX), f32),
        in_specs=[hbm] * 6 + [pl.BlockSpec(memory_space=pltpu.SMEM)],
        out_specs=vmem,
        scratch_shapes=[
            pltpu.SMEM((NBLK,), jnp.int32),
            pltpu.VMEM((2, NY, 2 * NX), bf16),
            pltpu.VMEM((2, NY, NX), f32),
            pltpu.VMEM((4, NY, NX), f32),
            pltpu.VMEM((2, 2, NBLK * SB), f32),
            pltpu.VMEM((2, 2, NBLK * SB), f32),
            pltpu.VMEM((rb, NX), f32),
            pltpu.VMEM((16, NBLK * SB), bf16),
            pltpu.VMEM((16, NBLK * SB), bf16),
            pltpu.VMEM((2, 256, 768), bf16),
            pltpu.VMEM((2, 512, 384), bf16),
            pltpu.VMEM((4, 512, NX), f32),
            pltpu.VMEM((2, 384, 256), bf16),
            pltpu.VMEM((2, 768, 256), bf16),
            pltpu.VMEM((2, 128, 256), bf16),
            pltpu.VMEM((2, 256, SB), bf16),
            pltpu.VMEM((256, SB), f32),
            pltpu.VMEM((128, SB), f32),
            pltpu.VMEM((128, SB), f32),
            pltpu.VMEM((128, SB), f32),
            pltpu.VMEM((64, SB), f32),
            pltpu.VMEM((64, SB), f32),
            pltpu.VMEM((nb - 1, 64, SB), f32),
            pltpu.VMEM((64, SB), f32),
            pltpu.VMEM((NY, NX), f32),
            pltpu.VMEM((NY, NX), f32),
            pltpu.VMEM((2, nr - 1, rb // 2, NX), f32),
            pltpu.VMEM((2, nr - 1, rb // 2, NX), f32),
            pltpu.VMEM((2, 2, rb // 2, NX), f32),
            pltpu.VMEM((NY, NX), f32),
            pltpu.VMEM((rb + 16, 2 * NX), f32),
            pltpu.VMEM((2, rb, 2 * NX), f32),
            pltpu.VMEM((rb + 16, NX), f32),
            pltpu.VMEM((2, rb, NX), f32),
            pltpu.VMEM((rb, 2 * NX), f32),
            pltpu.VMEM((2, 2, SB), f32),
            pltpu.VMEM((64, 2, SB), f32),
            pltpu.SemaphoreType.DMA((25,)),
            pltpu.SemaphoreType.DMA((25,)),
            pltpu.SemaphoreType.DMA((6,)),
            pltpu.SemaphoreType.REGULAR,
        ],
        compiler_params=pltpu.CompilerParams(
            collective_id=0, has_side_effects=True, vmem_limit_bytes=48 * 1024 * 1024
        ),
    )(
        *(
            pltpu.with_memory_space_constraint(operand, pltpu.HBM)
            for operand in (
                coil_maps[0, 0],
                kspace_data[0],
                smooth_weight[0, 0],
                kernel_cols.T,
                kernel_rows.T,
                tile_index,
            )
        ),
        caipi_cycle,
    )
    return fields[0][None, None], fields[1][None, None]


def solution(mesh, split_grp=(4, 4)):
    dims = (mesh.shape["band"],) + tuple(split_grp) + (mesh.shape["row"],)
    return jax.shard_map(
        functools.partial(on_device, dims),
        mesh=mesh,
        in_specs=(
            P("grp", "row", None, None),
            P("band", "grp", "row", None, None),
            P("band", "grp", "row", None),
            P(),
            P(),
            P(),
            P("band"),
        ),
        out_specs=(P("band", "grp", "row", None), P("band", "grp", "row", None)),
        check_vma=False,
    )
```

```python
import functools
import math

import jax
import jax.numpy as jnp
from jax import lax
from jax.experimental import pallas as pl
from jax.experimental.pallas import tpu as pltpu
from jax.sharding import PartitionSpec as P

NY = 256
NX = 256
TY = 16
TX = 16
SB = 128
NBLK = 16
HALF = NX // 2

reg_strength = 0.5
damping = 1.0
f32 = jnp.float32
bf16 = jnp.bfloat16
MESH = pl.DeviceIdType.MESH


def cos_turn(n):
    n = n - 256.0 * jnp.floor(n * (1.0 / 256.0))
    t = (jnp.abs(n - 128.0) - 64.0) * (2.0 * math.pi / 256.0)
    u = t * t
    series = -1.0 / math.factorial(11)
    for order, sign in ((9, 1.0), (7, -1.0), (5, 1.0), (3, -1.0), (1, 1.0)):
        series = sign / math.factorial(order) + u * series
    return t * series


def sin_turn(n):
    return cos_turn(n + 192.0)


def split(x):
    high = x.astype(bf16)
    return high, (x - high.astype(f32)).astype(bf16)


def mm(a, b):
    return jnp.dot(a, b, preferred_element_type=f32)


def mm_nt(a, b):
    return lax.dot_general(a, b, (((1,), (1,)), ((), ())), preferred_element_type=f32)


def iota(shape, axis):
    return lax.broadcasted_iota(jnp.int32, shape, axis)


def kernel(
    dims,
    coil_hbm,
    ks_hbm,
    w_hbm,
    kc_hbm,
    kr_hbm,
    tile_hbm,
    caipi_ref,
    out_ref,
    tile_ref,
    coil_v,
    coil_send,
    coil_buf,
    ks_own,
    ks_part,
    w_ref,
    kc_v,
    kr_v,
    row_p,
    row_k,
    mixed_ref,
    col_q,
    col_f,
    kc_nt,
    kc_nn,
    kr2,
    v_in,
    v_ref,
    v_tot,
    pair_in,
    own_sum,
    band_in,
    own_tot,
    part1,
    part2,
    rs1,
    rs2,
    gsum,
    rg,
    vext,
    vgrp,
    wext,
    wgrp,
    lap_ref,
    sc_out,
    sc_in,
    ssem,
    rsem,
    lsem,
    hello,
):
    nb, ny, nz, nr = dims
    ng = ny * nz
    nl = nr // 2
    rb = NY // nr
    b = lax.axis_index("band")
    g = lax.axis_index("grp")
    r = lax.axis_index("row")
    h = lax.rem(r, 2)
    zl = lax.div(r, 2)
    gy = lax.div(g, nz)
    gz = lax.rem(g, nz)
    partner = {"row": r + 1 - 2 * h}
    band_peer = [{"band": lax.rem(b + o, nb)} for o in range(1, nb)]
    plane_peer = [
        {
            "band": lax.rem(b + i, nb),
            "grp": lax.rem(gy + j, ny) * nz + gz,
            "row": zl * 2 + lax.rem(h + k, 2),
        }
        for i in range(nb)
        for j in range(ny)
        for k in range(2)
        if i or j or k
    ]
    line = gz * nl + zl
    line_peer = []
    for o in range(1, nz * nl):
        at = lax.rem(line + o, nz * nl)
        line_peer.append({"grp": gy * nz + lax.div(at, nl), "row": lax.rem(at, nl) * 2 + h})
    g_next = {"grp": lax.rem(g + 1, ng)}
    g_prev = {"grp": lax.rem(g + ng - 1, ng)}
    across = [{"row": lax.rem(zl + o, nl) * 2 + 1 - h} for o in range(1, nl)]
    across = [{"row": lax.rem(zl + o, nl) * 2 + 1 - h} for o in range(1, nl)]
    size = nz * nl
    reach = size // 4
    near_line = [line_peer[o - 1] for o in range(1, size) if min(o, size - o) <= reach]
    hello_peer = [line_peer[reach - 1], line_peer[size - reach - 1]]
    peers = [g_next, g_prev] + near_line[reach - 1 : reach + 1] + plane_peer[::-1] + near_line[: reach - 1] + near_line[reach + 1 :] + across

    barrier = pltpu.get_barrier_semaphore()
    for peer in peers:
        pl.semaphore_signal(barrier, inc=1, device_id=peer, device_id_type=MESH)
    fetches = [
        pltpu.make_async_copy(src, dst, lsem.at[at])
        for at, (src, dst) in enumerate(
            (
                (tile_hbm, tile_ref),
                (kc_hbm, kc_v),
                (kr_hbm, kr_v),
                (ks_hbm, ks_own),
                (coil_hbm, coil_v),
                (w_hbm, w_ref),
            )
        )
    ]
    for copy in fetches:
        copy.start()

    slots = iter(range(64))

    def exchange(copies, sized):
        slot = next(slots)
        for src, dst, peer in copies:
            pltpu.make_async_remote_copy(
                src_ref=src,
                dst_ref=dst,
                send_sem=ssem.at[slot],
                recv_sem=rsem.at[slot],
                device_id=peer,
                device_id_type=MESH,
            ).start()
        whole = pltpu.make_async_remote_copy(
            src_ref=sized,
            dst_ref=sized,
            send_sem=ssem.at[slot],
            recv_sem=rsem.at[slot],
            device_id=partner,
            device_id_type=MESH,
        )
        started.append(whole)
        return whole

    started = []

    def send(src, dst, peer):
        return exchange([(src, dst, peer)], dst)

    hb = rb // 2

    def row_at_place(place):
        inside = jnp.bitwise_and(place, 127)
        return (
            lax.shift_right_logical(inside, hb.bit_length() - 1) * rb
            + lax.shift_right_logical(place, 7) * hb
            + jnp.bitwise_and(inside, hb - 1)
        )

    lane = iota((1, 256), 1)
    lane_f = lax.shift_right_logical(jnp.bitwise_and(lane, 127), 3).astype(f32)
    lane_m = jnp.zeros((1, 256), f32)
    lane_c = jnp.bitwise_and(lane, 15).astype(f32)
    row_block = jnp.bitwise_and(lane, 7) + 8 * lax.shift_right_logical(lane, 7)
    col_block = lax.shift_right_logical(lane, 4)
    q_half = (iota((16, HALF), 1) + h * HALF).astype(f32)
    p_lane = row_at_place(iota((16, 256), 1)).astype(f32)
    sub16_q = iota((16, HALF), 0).astype(f32)
    sub = iota((16, 256), 0)
    sub_block = jnp.bitwise_and(sub, 7)
    sub_row = lax.shift_right_logical(sub, 3).astype(f32)
    scale = 1.0 / 16.0
    fetches[0].wait()
    cycle = caipi_ref[0]
    for half in range(2):
        for k in range(half * 8, half * 8 + 8):
            tile = tile_ref[k]
            ty = jnp.right_shift(tile, 4).astype(f32) * 16.0
            tx = jnp.bitwise_and(tile, 15).astype(f32) * 16.0
            turns = 256.0 - 64.0 * jnp.bitwise_and(cycle * k, 3).astype(f32)
            lane_f = jnp.where(row_block == k, lane_f + ty, lane_f)
            lane_m = jnp.where(row_block == k, turns, lane_m)
            lane_c = jnp.where(col_block == k, lane_c + tx, lane_c)
            turn = q_half * (sub16_q + tx)
            at = (k % 8) * 16
            for part, values in ((0, cos_turn(turn)), (1, sin_turn(turn))):
                high, low = split(values * scale)
                to = slice(part * HALF, part * HALF + HALF)
                col_q[half, at : at + 16, to] = high
                col_q[half, 128 + at : 128 + at + 16, to] = low
                col_q[half, 256 + at : 256 + at + 16, to] = high
    turn = row_at_place(iota((256, 256), 0)).astype(f32) * lane_f + lane_m
    for part, values in ((0, cos_turn(turn)), (1, sin_turn(turn))):
        high, low = split(values * scale)
        row_p[part, :, 0:256] = high
        row_p[part, :, 256:512] = high
        row_p[part, :, 512:768] = low
    fetches[1].wait()
    fetches[2].wait()
    for k in range(NBLK):
        half, at = k // 8, (k % 8) * 16
        cols = slice(k * SB, k * SB + SB)
        piece = kc_v[:, cols]
        kc_nt[half, at : at + 16, 0:SB] = piece
        kc_nt[half, at : at + 16, SB : 2 * SB] = piece
        kc_nn[half, at : at + 16, :] = piece
        kc_nn[half, 128 + at : 128 + at + 16, :] = piece
        kr2[pl.ds(half * 128 + k % 8, 16, stride=8), :] = kr_v[:, cols].astype(f32)
    keep = (
        jnp.bitwise_and(iota((128, 128), 0), 7)
        == lax.shift_right_logical(iota((128, 128), 1), 4)
    )
    keep4 = jnp.concatenate([keep] * 4, axis=0)

    def spread(ref, first):
        halves = range(2)
        spreads = []
        for half in halves:
            weights = kr2[half * 128 : half * 128 + 128, :].reshape(16, 8, SB)
            pieces = []
            for at in range(4):
                at = (first * 2 + at) * NBLK + half * 8
                pieces.append((weights * ref[at : at + 8, :][None]).reshape(128, SB))
            spreads.append(jnp.concatenate(split(jnp.concatenate(pieces, axis=0)), axis=1))
        tiles = [mm_nt(spreads[half], kc_nt[half]) for half in halves]
        parts = [split(jnp.where(keep4, tiles[half], 0.0)) for half in halves]
        mixed = [
            mm(jnp.concatenate([high, high, low], axis=1), col_q[half])
            for half, (high, low) in zip(halves, parts)
        ]
        blocks = [[], []]
        for half in halves:
            for c in range(2):
                real = mixed[half][c * 256 : c * 256 + 128]
                imag = mixed[half][c * 256 + 128 : c * 256 + 256]
                blocks[c].append(
                    jnp.concatenate(
                        [real[:, :HALF] - imag[:, HALF:], real[:, HALF:] + imag[:, :HALF]], axis=1
                    )
                )
        factors = []
        for c in range(2):
            high, low = split(jnp.concatenate(blocks[c], axis=0))
            factors.append(jnp.concatenate([high, low, high], axis=0))
        return factors

    def row_stage(factors, sub, first=0, start=None):
        rows = slice(sub * 128, sub * 128 + 128)
        left = jnp.concatenate([row_p[0, rows, :], row_p[1, rows, :]], axis=0)
        sum_r, sum_i = (None, None) if start is None else (start[:, :HALF], start[:, HALF:])
        for c, factor in enumerate(factors, first):
            mixed = mm(left, factor)
            im_r = mixed[:128, :HALF] - mixed[128:, HALF:]
            im_i = mixed[:128, HALF:] + mixed[128:, :HALF]
            coil_r, coil_i = coil_buf[c, rows, :HALF], coil_buf[c, rows, HALF:]
            term_r = coil_r * im_r + coil_i * im_i
            term_i = coil_r * im_i - coil_i * im_r
            sum_r = term_r if sum_r is None else sum_r + term_r
            sum_i = term_i if sum_i is None else sum_i + term_i
        return jnp.concatenate([sum_r, sum_i], axis=1)

    def by_block(samples, base):
        for c in range(2):
            for ch in range(2):
                for k in range(NBLK):
                    at = ((base + c) * 2 + ch) * NBLK + k
                    v_in[at : at + 1, :] = samples[c, ch : ch + 1, k * SB : k * SB + SB]

    nq = nr // 2
    near_base = lax.div(r, nq) * nq
    order = [(nq - near_base, i) for i in range(nq)] + [(near_base, i) for i in range(1, nq)]
    targets = [base + lax.rem(lax.rem(r, nq) + i, nq) for base, i in order]
    crossed = [i % 2 for _, i in order]

    def place_of(block, sub):
        return pl.ds(pl.multiple_of(sub * 128 + block * hb, hb), hb)

    def scatter(part, slots_in, sub):
        return exchange(
            [
                (part.at[place_of(to, sub)], slots_in.at[sub, o], {"row": to})
                for o, to in enumerate(targets)
            ],
            slots_in.at[sub, pl.ds(0, nr - 1)],
        )

    def collect(part, slots_in, sub):
        sums = [part[place_of(r, sub), :], None]
        for o, other in enumerate(crossed):
            piece = slots_in[sub, o]
            sums[other] = piece if sums[other] is None else sums[other] + piece
        same, diff = sums
        return same, diff

    def widen(same, diff):
        even = h == 0
        return (
            jnp.where(even, same[:, :HALF], diff[:, :HALF]),
            jnp.where(even, diff[:, :HALF], same[:, :HALF]),
            jnp.where(even, same[:, HALF:], diff[:, HALF:]),
            jnp.where(even, diff[:, HALF:], same[:, HALF:]),
        )


    fetches[3].wait()
    by_block(ks_own, 0)
    fetches[4].wait()

    def half_of(part, half):
        return pl.ds(pl.multiple_of(part * NX + half * HALF, HALF), HALF)

    for c in range(2):
        for part in range(2):
            to = slice(part * HALF, part * HALF + HALF)
            for place in range(0, NY, hb):
                block, sub = (place % 128) // hb, place // 128
                rows, at = slice(place, place + hb), slice(block * rb + sub * hb, block * rb + sub * hb + hb)
                coil_send[c, rows, to] = coil_v[c, at, half_of(part, 1 - h)].astype(f32)
                coil_buf[c, rows, to] = coil_v[c, at, half_of(part, h)].astype(f32)
    factors = spread(v_in, 0)
    for sub in range(2):
        part1[sub * 128 : sub * 128 + 128, :] = row_stage(factors, sub)
    fetches[5].wait()
    wext[8 : 8 + rb, :] = w_ref[...]

    pl.semaphore_wait(barrier, len(peers))

    ks_copy = send(ks_own, ks_part, partner)
    partner_coils = send(coil_send, coil_buf.at[pl.ds(2, 2)], partner)
    row_next = {"row": lax.rem(r + 1, nr)}
    row_prev = {"row": lax.rem(r + nr - 1, nr)}
    w_copies = exchange(
        [
            (w_ref.at[pl.ds(0, hb)], wgrp.at[1, pl.ds(0, hb)], g_prev),
            (w_ref.at[pl.ds(hb, hb)], wgrp.at[0, pl.ds(hb, hb)], g_next),
            (w_ref.at[pl.ds(rb - 8, 8)], wext.at[pl.ds(0, 8)], row_next),
            (w_ref.at[pl.ds(0, 8)], wext.at[pl.ds(rb + 8, 8)], row_prev),
        ],
        wext,
    )
    for peer in hello_peer:
        pl.semaphore_signal(hello, inc=1, device_id=peer, device_id_type=MESH)
    ks_copy.wait_recv()
    by_block(ks_part, 2)
    factors = spread(v_in, 2)
    partner_coils.wait_recv()
    part1[0:128, :] = row_stage(factors, 0, 2, part1[0:128, :])
    scattered = [scatter(part1, rs1, 0)]
    part1[128:256, :] = row_stage(factors, 1, 2, part1[128:256, :])
    scattered.append(scatter(part1, rs1, 1))
    for half in range(2):
        sub_f = sub_row
        sub_m = jnp.zeros((16, 256), f32)
        for k in range(half * 8, half * 8 + 8):
            ty = jnp.right_shift(tile_ref[k], 4).astype(f32) * 16.0
            turns = 256.0 - 64.0 * jnp.bitwise_and(cycle * k, 3).astype(f32)
            sub_f = jnp.where(sub_block == k % 8, sub_f + ty, sub_f)
            sub_m = jnp.where(sub_block == k % 8, turns, sub_m)
        for y in range(0, 16, 2):
            turn = p_lane * (sub_f + float(y)) + sub_m
            for part, values in ((0, cos_turn(turn)), (1, sin_turn(turn))):
                high, low = split(values * scale)
                at = part * 256 + half * 128 + y * 8
                for sub_at in range(2):
                    cols = slice(sub_at * 128, sub_at * 128 + 128)
                    row_k[sub_at, at : at + 16, 0:128] = high[:, cols]
                    row_k[sub_at, at : at + 16, 128:256] = high[:, cols]
                    row_k[sub_at, at : at + 16, 256:384] = low[:, cols]
    turn = (iota((HALF, 256), 0) + h * HALF).astype(f32) * lane_c
    cosine, sine = cos_turn(turn) * scale, sin_turn(turn) * scale
    levels = tuple(zip(split(cosine), split(sine)))
    for third, level in enumerate((0, 1, 0)):
        cos_part, sin_part = levels[level]
        at = third * 256
        for half in range(2):
            cols = slice(half * 128, half * 128 + 128)
            col_f[half, at : at + 128, 0:128] = cos_part[:, cols]
            col_f[half, at : at + 128, 128:256] = -sin_part[:, cols]
            col_f[half, at + 128 : at + 256, 0:128] = sin_part[:, cols]
            col_f[half, at + 128 : at + 256, 128:256] = cos_part[:, cols]
    gathered = []
    for sub in range(2):
        scattered[sub].wait_recv()
        same, diff = collect(part1, rs1, sub)
        gsum[sub, 0] = same
        gsum[sub, 1] = diff
        gathered.append(
            exchange(
                [
                    (gsum.at[sub, crossed[o]], rg.at[place_of(r, sub)], {"row": to})
                    for o, to in enumerate(targets)
                ],
                rg.at[pl.ds(0, (nr - 1) * hb)],
            )
        )
        rg[place_of(r, sub), :] = same
        for at, piece in enumerate(widen(same, diff)):
            vext[8 + sub * hb : 8 + sub * hb + hb, at * HALF : at * HALF + HALF] = piece
    def frequencies(c, sub):
        rows = slice(sub * 128, sub * 128 + 128)
        coil_r, coil_i = coil_buf[c, rows, :HALF], coil_buf[c, rows, HALF:]
        image_r, image_i = rg[rows, :HALF], rg[rows, HALF:]
        high, low = split(
            jnp.concatenate(
                [coil_r * image_r - coil_i * image_i, coil_r * image_i + coil_i * image_r], axis=1
            )
        )
        return mm(row_k[sub], jnp.concatenate([high, low, high], axis=0))

    gathered[0].wait_recv()
    for c in range(4):
        mixed_ref[c] = frequencies(c, 0)
    gathered[1].wait_recv()
    v_copies = exchange(
        [
            (vext.at[pl.ds(8, hb)], vgrp.at[1, pl.ds(0, hb)], g_prev),
            (vext.at[pl.ds(8 + hb, hb)], vgrp.at[0, pl.ds(hb, hb)], g_next),
            (vext.at[pl.ds(rb, 8)], vext.at[pl.ds(0, 8)], row_next),
            (vext.at[pl.ds(8, 8)], vext.at[pl.ds(rb + 8, 8)], row_prev),
        ],
        vext,
    )

    for first in (2, 0):
        lefts = []
        for c in (first, first + 1):
            mixed = mixed_ref[c] + frequencies(c, 1)
            high, low = split(
                jnp.concatenate(
                    [
                        mixed[:256, :HALF] + mixed[256:, HALF:],
                        mixed[:256, HALF:] - mixed[256:, :HALF],
                    ],
                    axis=1,
                )
            )
            lefts.append(jnp.concatenate([high, high, low], axis=1))
        grids = [
            mm(
                jnp.concatenate([left[half * 128 : half * 128 + 128] for left in lefts], axis=0),
                col_f[half],
            )
            for half in range(2)
        ]
        sampled = []
        for half in range(2):
            parts = [
                grids[half][c * 128 : c * 128 + 128, ch * 128 : ch * 128 + 128]
                for c in range(2)
                for ch in range(2)
            ]
            high, low = split(jnp.where(keep4, jnp.concatenate(parts, axis=0), 0.0))
            sampled.append(mm(jnp.concatenate([high, low], axis=1), kc_nn[half]))
        for half in range(2):
            weights = kr2[half * 128 : half * 128 + 128, :]
            for at in range(4):
                weighted = sampled[half][at * 128 : at * 128 + 128] * weights
                to = (first * 2 + at) * NBLK + half * 8
                v_ref[to : to + 8, :] = jnp.sum(weighted.reshape(16, 8, SB), axis=0)
        if first == 2:
            pair = send(v_ref.at[pl.ds(64, 64)], pair_in, partner)
    pair.wait_recv()
    own_sum[...] = v_ref[0:64, :] + pair_in[...]
    bands = exchange(
        [(own_sum, band_in.at[o], peer) for o, peer in enumerate(band_peer)],
        band_in.at[pl.ds(0, nb - 1)],
    )

    late_copies = [
        exchange(
            [
                (w_ref.at[pl.ds(hb, hb)], wgrp.at[1, pl.ds(hb, hb)], g_prev),
                (w_ref.at[pl.ds(0, hb)], wgrp.at[0, pl.ds(0, hb)], g_next),
            ],
            w_ref,
        ),
        exchange(
            [
                (vext.at[pl.ds(8 + hb, hb)], vgrp.at[1, pl.ds(hb, hb)], g_prev),
                (vext.at[pl.ds(8, hb)], vgrp.at[0, pl.ds(0, hb)], g_next),
            ],
            lap_ref,
        ),
    ]

    def stage_start(index, base, value, stage_peers):
        sc_out[index] = value
        return exchange(
            [(sc_out.at[index], sc_in.at[base + o], peer) for o, peer in enumerate(stage_peers)],
            sc_in.at[pl.ds(base, len(stage_peers))],
        )

    def stage_end(base, value, copies, count):
        copies.wait_recv()
        return value + jnp.sum(sc_in[base : base + count], axis=0)

    bands.wait_recv()
    tot = own_sum[...]
    for o in range(nb - 1):
        tot = tot + band_in[o]
    own_tot[...] = tot
    back = send(own_tot, v_tot.at[pl.ds(64, 64)], partner)
    v_tot[0:64, :] = tot
    squares = jnp.sum(tot * tot, axis=0, keepdims=True) * (1.0 / nb)

    w_copies.wait_recv()
    v_copies.wait_recv()
    w = w_ref[...]
    row_at = iota((rb, NX), 0)
    col_at = iota((rb, NX), 1)
    zero = jnp.zeros((rb, NX), f32)
    w_up = jnp.where((row_at == 0) & (r == 0), zero, wext[7 : 7 + rb, :])
    w_down = jnp.where((row_at == rb - 1) & (r == nr - 1), zero, wext[9 : 9 + rb, :])
    w_left = jnp.where(col_at == 0, zero, pltpu.roll(w, 1, 1))
    w_right = jnp.where(col_at == NX - 1, zero, pltpu.roll(w, NX - 1, 1))
    part = zero[:hb]
    w_next_edge = jnp.where(g == ng - 1, part, wgrp[1, :hb])
    w_prev_edge = jnp.where(g == 0, part, wgrp[0, hb:])
    power = jnp.zeros((1, 2 * SB), f32)
    energy = jnp.zeros((1, 2 * SB), f32)
    for ch in range(2):
        cols = slice(ch * NX, ch * NX + NX)
        v = vext[8 : 8 + rb, cols]
        total = w_up * (v - vext[7 : 7 + rb, cols])
        total += w_down * (v - vext[9 : 9 + rb, cols])
        total += w_left * (v - pltpu.roll(v, 1, 1))
        total += w_right * (v - pltpu.roll(v, NX - 1, 1))
        smoothed = reg_strength * (w * total) + damping * v
        lap_ref[:, cols] = smoothed
        power = power + jnp.sum(v * v, axis=0, keepdims=True)
        energy = energy + jnp.sum(v * smoothed, axis=0, keepdims=True)
        step = v[:hb] - vgrp[1, :hb, cols]
        edges = jnp.sum(w[:hb] * w_next_edge * (step * step), axis=0, keepdims=True)
        step = v[hb:] - vgrp[0, hb:, cols]
        edges += jnp.sum(w[hb:] * w_prev_edge * (step * step), axis=0, keepdims=True)
        energy = energy + reg_strength * edges
    power = power[:, :SB] + power[:, SB:]
    energy = energy[:, :SB] + energy[:, SB:]
    first_row = iota((2, SB), 0) == 0
    tile_sum = jnp.where(first_row, power, energy)
    tile_sum = tile_sum + jnp.where(first_row, 0.0, squares)
    plane = stage_start(0, 0, tile_sum, plane_peer)
    factors = spread(v_tot, 0)
    back.wait_recv()
    factors += spread(v_tot, 2)
    part2[0:128, :] = row_stage(factors, 0)
    scattered = [scatter(part2, rs2, 0)]
    part2[128:256, :] = row_stage(factors, 1)
    scattered.append(scatter(part2, rs2, 1))
    tile_sum = stage_end(0, tile_sum, plane, len(plane_peer))
    pl.semaphore_wait(hello, len(hello_peer))
    along = stage_start(1, len(plane_peer), tile_sum, line_peer)
    for copy in late_copies:
        copy.wait_recv()
    w_prev = jnp.where(g == 0, zero, wgrp[0])
    w_next = jnp.where(g == ng - 1, zero, wgrp[1])
    for ch in range(2):
        cols = slice(ch * NX, ch * NX + NX)
        v = vext[8 : 8 + rb, cols]
        total = w_prev * (v - vgrp[0, :, cols]) + w_next * (v - vgrp[1, :, cols])
        lap_ref[:, cols] += reg_strength * (w * total)
    for copy in scattered:
        copy.wait_recv()
    tile_sum = stage_end(len(plane_peer), tile_sum, along, len(line_peer))
    totals = jnp.sum(tile_sum, axis=1, keepdims=True)
    alpha = totals[0:1] / totals[1:2]
    for sub in range(2):
        rows = slice(sub * hb, sub * hb + hb)
        for at, piece in enumerate(widen(*collect(part2, rs2, sub))):
            cols = slice(at * HALF, at * HALF + HALF)
            v = vext[8 + sub * hb : 8 + sub * hb + hb, cols]
            out_ref[0, rows, cols] = alpha * v
            out_ref[1, rows, cols] = v - alpha * (piece + lap_ref[rows, cols])
    for copy in started:
        copy.wait_send()


def on_device(
    dims, kspace_data, coil_maps, smooth_weight, kernel_cols, kernel_rows, tile_index, caipi_cycle
):
    nb, ny, nz, nr = dims
    rb = NY // nr
    vmem = pl.BlockSpec(memory_space=pltpu.VMEM)
    hbm = pl.BlockSpec(memory_space=pltpu.HBM)
    fields = pl.pallas_call(
        functools.partial(kernel, dims),
        out_shape=jax.ShapeDtypeStruct((2, rb, 2 * NX), f32),
        in_specs=[hbm] * 6 + [pl.BlockSpec(memory_space=pltpu.SMEM)],
        out_specs=vmem,
        scratch_shapes=[
            pltpu.SMEM((NBLK,), jnp.int32),
            pltpu.VMEM((2, NY, 2 * NX), bf16),
            pltpu.VMEM((2, NY, NX), f32),
            pltpu.VMEM((4, NY, NX), f32),
            pltpu.VMEM((2, 2, NBLK * SB), f32),
            pltpu.VMEM((2, 2, NBLK * SB), f32),
            pltpu.VMEM((rb, NX), f32),
            pltpu.VMEM((16, NBLK * SB), bf16),
            pltpu.VMEM((16, NBLK * SB), bf16),
            pltpu.VMEM((2, 256, 768), bf16),
            pltpu.VMEM((2, 512, 384), bf16),
            pltpu.VMEM((4, 512, NX), f32),
            pltpu.VMEM((2, 384, 256), bf16),
            pltpu.VMEM((2, 768, 256), bf16),
            pltpu.VMEM((2, 128, 256), bf16),
            pltpu.VMEM((2, 256, SB), bf16),
            pltpu.VMEM((256, SB), f32),
            pltpu.VMEM((128, SB), f32),
            pltpu.VMEM((128, SB), f32),
            pltpu.VMEM((128, SB), f32),
            pltpu.VMEM((64, SB), f32),
            pltpu.VMEM((64, SB), f32),
            pltpu.VMEM((nb - 1, 64, SB), f32),
            pltpu.VMEM((64, SB), f32),
            pltpu.VMEM((NY, NX), f32),
            pltpu.VMEM((NY, NX), f32),
            pltpu.VMEM((2, nr - 1, rb // 2, NX), f32),
            pltpu.VMEM((2, nr - 1, rb // 2, NX), f32),
            pltpu.VMEM((2, 2, rb // 2, NX), f32),
            pltpu.VMEM((NY, NX), f32),
            pltpu.VMEM((rb + 16, 2 * NX), f32),
            pltpu.VMEM((2, rb, 2 * NX), f32),
            pltpu.VMEM((rb + 16, NX), f32),
            pltpu.VMEM((2, rb, NX), f32),
            pltpu.VMEM((rb, 2 * NX), f32),
            pltpu.VMEM((2, 2, SB), f32),
            pltpu.VMEM((64, 2, SB), f32),
            pltpu.SemaphoreType.DMA((17,)),
            pltpu.SemaphoreType.DMA((17,)),
            pltpu.SemaphoreType.DMA((6,)),
            pltpu.SemaphoreType.REGULAR,
        ],
        compiler_params=pltpu.CompilerParams(
            collective_id=0, has_side_effects=True, vmem_limit_bytes=48 * 1024 * 1024
        ),
    )(
        *(
            pltpu.with_memory_space_constraint(operand, pltpu.HBM)
            for operand in (
                coil_maps[0, 0],
                kspace_data[0],
                smooth_weight[0, 0],
                kernel_cols.T,
                kernel_rows.T,
                tile_index,
            )
        ),
        caipi_cycle,
    )
    return fields[0][None, None], fields[1][None, None]


def solution(mesh, split_grp=(4, 4)):
    dims = (mesh.shape["band"],) + tuple(split_grp) + (mesh.shape["row"],)
    return jax.shard_map(
        functools.partial(on_device, dims),
        mesh=mesh,
        in_specs=(
            P("grp", "row", None, None),
            P("band", "grp", "row", None, None),
            P("band", "grp", "row", None),
            P(),
            P(),
            P(),
            P("band"),
        ),
        out_specs=(P("band", "grp", "row", None), P("band", "grp", "row", None)),
        check_vma=False,
    )
```
